32 devices in a mesh: group: 2 (over y), mx: 4 (over x, core), my: 4 (over z).
Axes of the slice: x: 2, y: 2, z: 4, core: 2. Of those that a mesh axis runs over, the one named last changes fastest.
Arguments:
- teacher_feats: bfloat16 [256, 64, 6144], P(None, ('group', 'my'), 'mx'), parts along dimension 1, may hold values from -6 to 6
- t_gain: bfloat16 [6144], P('mx'), may hold values from 0.25 to 1.75
- t_bias: bfloat16 [6144], P('mx'), may hold values from -3 to 3
- projection: bfloat16 [6144, 1408], P('mx'), may hold values from -0.078125 to 0.078125
- student_in: bfloat16 [256, 64, 1408], P('mx', ('group', 'my')), parts along dimension 1, may hold values from -6 to 6
- s_gain: float32 [1408], replicated, may hold values from 0.25 to 1.75
- w_in: bfloat16 [1408, 6144], P('mx', 'my'), may hold values from -0.15625 to 0.15625
- w_out: bfloat16 [6144, 1408], P('my', 'mx'), may hold values from -0.078125 to 0.078125
Outputs:
- mse_loss: float32 [2], P('group'), parts along dimension 0
- grad_in: float32 [2816, 6144], P(('group', 'mx'), 'my'), parts along dimension 0
- grad_out: float32 [12288, 1408], P(('group', 'my'), 'mx'), parts along dimension 0
The draws below stay inside these ranges and needn't reach their ends.
There are 2 independent parts, one for each index of `group`. The reference program is written for one: setup_inputs(seed, part) draws one part's arguments, and reference() takes and returns one part's arrays. A program takes and returns all parts, laid end to end along the dimension named above; an argument that names none is the same for every part. Nothing has to cross between parts.
All inputs are finite; a program needn't handle non-finite values.
Results may differ from the reference program's by a relative error of at most 0.011.
Values may be sent and summed in bfloat16 or wider, within the bound.
No kernel may reach another device: no remote copies, remote signals or barrier semaphores. Data moves between devices by JAX's collectives and lax.ppermute only.
A program may use at most 192 MiB of HBM per device.

```python
import jax
import jax.numpy as jnp
from jax import lax

DT = 6144
DS = 1408
FS = 6144
PATCHES = 256
IMAGES = 32
N_MX = 4
N_MY = 4


def strengthened(array, key, source, target, blocks, factor):
    def block_of(axis_at):
        return (jnp.arange(array.shape[axis_at]) // (array.shape[axis_at] // blocks)).reshape((-1,) + (1,) * (array.ndim - 1 - axis_at))

    near = jax.random.permutation(key, blocks)[block_of(target)]
    far = (block_of(target) + blocks // 2) % blocks
    return jnp.where((block_of(source) == near) | (block_of(source) == far), factor * array, array)


def level_of(key, shape, cuts, low, largest):
    def one(position, shards_of):
        heights = jax.random.uniform(jax.random.fold_in(jax.random.fold_in(key, 6), position), (shards_of,), jnp.float32, low / len(cuts), largest / len(cuts))
        return jnp.repeat(jnp.exp(heights), shape[position] // shards_of).reshape((-1,) + (1,) * (len(shape) - position - 1))

    level = one(*cuts[0])
    for cut in cuts[1:]:
        level = level * one(*cut)
    return level


def scatter_about(stream_key, dims, width, most, shards=(), held_as=jnp.bfloat16):
    array = width * jax.random.normal(stream_key, dims, jnp.float32)
    if shards:
        array = array * level_of(stream_key, dims, shards, -0.22, 0.18)
    return jnp.clip(array, -most, most).astype(held_as)


def gaussian_with(own_key, dims, deviation, limit, split, heavy, dtype=jnp.bfloat16):
    array = deviation * jax.random.normal(own_key, dims, jnp.float32)
    if split:
        array = array * level_of(own_key, dims, split, -0.22, 0.18)
    return jnp.clip(strengthened(array, jax.random.fold_in(own_key, 3), *heavy), -limit, limit).astype(dtype)


def setup_inputs(seed: int = 0, part: int = 0) -> dict:
    arg_keys = jax.random.split(jax.random.key(seed), 9)
    part_keys = jax.random.split(jax.random.fold_in(arg_keys[8], part), 9)
    teacher_feats = scatter_about(part_keys[0], (PATCHES, IMAGES, DT), 1.0, 6.0, ((1, 4), (2, 4)))
    t_gain = jnp.clip(1.0 + 0.15 * jax.random.normal(arg_keys[1], (DT,), jnp.float32), 0.25, 1.75).astype(jnp.bfloat16)
    t_bias = scatter_about(arg_keys[2], (DT,), 0.5, 3.0, ((0, 4),))
    projection = scatter_about(arg_keys[3], (DT, DS), DT ** -0.5, 0.078125, ((0, 4),))
    student_in = gaussian_with(part_keys[4], (PATCHES, IMAGES, DS), 1.0, 6.0, ((0, 4), (1, 4)), (0, 2, 4, 2.0))
    s_gain = jnp.clip(1.0 + 0.15 * jax.random.normal(arg_keys[5], (DS,), jnp.float32), 0.25, 1.75)
    w_in = scatter_about(arg_keys[6], (DS, FS), DS ** -0.5, 0.15625, ((0, 4), (1, 4)))
    w_out = scatter_about(arg_keys[7], (FS, DS), FS ** -0.5, 0.078125, ((0, 4), (1, 4)))
    return {"teacher_feats": teacher_feats, "t_gain": t_gain, "t_bias": t_bias, "projection": projection, "student_in": student_in, "s_gain": s_gain, "w_in": w_in, "w_out": w_out}


def matmul(left, right):
    return jnp.dot(left.astype(jnp.float32), right.astype(jnp.float32), preferred_element_type=jnp.float32)

def gelu_value(value):
    return 0.5 * value * (1.0 + lax.erf(value * 0.7071067811865476))

def gelu_slope(value):
    return 0.5 * (1.0 + lax.erf(value * 0.7071067811865476)) + value * jnp.exp(-0.5 * value * value) * 0.3989422804014327

def reference(teacher_feats, t_gain, t_bias, projection, student_in, s_gain, w_in, w_out):
    tokens = PATCHES * IMAGES
    features = teacher_feats.reshape(tokens, DT).astype(jnp.float32)
    row_mean = lax.optimization_barrier(jnp.sum(features, axis=1, keepdims=True)) / DT
    row_square = lax.optimization_barrier(jnp.sum(features * features, axis=1, keepdims=True)) / DT
    tnorm = ((features - row_mean) * lax.rsqrt(row_square - row_mean * row_mean + 1e-06) * t_gain.astype(jnp.float32) + t_bias.astype(jnp.float32)).astype(jnp.bfloat16)
    target = matmul(tnorm, projection)
    student_f32 = student_in.reshape(tokens, DS).astype(jnp.float32)
    student_mean = lax.optimization_barrier(jnp.sum(student_f32, axis=1, keepdims=True)) / DS
    student_square = lax.optimization_barrier(jnp.sum(student_f32 * student_f32, axis=1, keepdims=True)) / DS
    normed = ((student_f32 - student_mean) * lax.rsqrt(student_square - student_mean * student_mean + 1e-06) * s_gain).astype(jnp.bfloat16)
    preact = matmul(normed, w_in)
    activation = gelu_value(preact).astype(jnp.bfloat16)
    block_size = FS // N_MY
    branch = jnp.zeros((tokens, DS), jnp.float32)
    for block in range(N_MY):
        low = block * block_size
        branch = branch + matmul(activation[:, low:low + block_size], w_out[low:low + block_size]).astype(jnp.bfloat16).astype(jnp.float32)
    residue = student_f32 + branch - target
    mse_loss = jnp.reshape(jnp.sum(residue * residue) / (tokens * DS), (1,))
    grad_output = (residue / jnp.sqrt(jnp.float32(tokens))).astype(jnp.bfloat16)
    grad_act = matmul(grad_output, w_out.T)
    grad_pre = (grad_act * gelu_slope(preact)).astype(jnp.bfloat16)
    row_span = tokens // N_MX
    grad_in = jnp.zeros((DS, FS), jnp.float32)
    grad_out = jnp.zeros((FS, DS), jnp.float32)
    for block in range(N_MX):
        low = block * row_span
        grad_in = grad_in + matmul(normed[low:low + row_span].T, grad_pre[low:low + row_span]).astype(jnp.bfloat16).astype(jnp.float32)
        grad_out = grad_out + matmul(activation[low:low + row_span].T, grad_output[low:low + row_span]).astype(jnp.bfloat16).astype(jnp.float32)
    return (mse_loss, grad_in, grad_out)
```

```python
import jax
import jax.numpy as jnp
from jax import lax
from jax.experimental import pallas as pl
from jax.experimental.pallas import tpu as pltpu
from jax.sharding import PartitionSpec as P

DT = 6144
DS = 1408
PATCHES = 256
F32 = jnp.float32
BF16 = jnp.bfloat16

epsilon = 1e-06


def gelu_value(value):
    return 0.5 * value * (1.0 + lax.erf(value * 0.7071067811865476))


def gelu_slope(value):
    return (
        0.5 * (1.0 + lax.erf(value * 0.7071067811865476))
        + value * jnp.exp(-0.5 * value * value) * 0.3989422804014327
    )


def swap(value, axis, bit):
    count = lax.axis_size(axis)
    return lax.ppermute(value, axis, [(i, i ^ bit) for i in range(count)])


def assemble_body(offs_ref, *refs):
    pieces, out, sems = refs[:-2], refs[-2], refs[-1]
    copies = []
    for i, piece in enumerate(pieces):
        off = pl.multiple_of(offs_ref[i], 16)
        copies.append(
            pltpu.make_async_copy(piece, out.at[pl.ds(off, piece.shape[0]), :], sems.at[i])
        )
    for copy in copies:
        copy.start()
    for copy in copies:
        copy.wait()


def assemble(pieces, offsets):
    cols = pieces[0].shape[1]
    rows = sum(p.shape[0] for p in pieces)
    offs = jnp.stack([jnp.asarray(o, jnp.int32) for o in offsets])
    return pl.pallas_call(
        assemble_body,
        out_shape=jax.ShapeDtypeStruct((rows, cols), pieces[0].dtype),
        in_specs=[pl.BlockSpec(memory_space=pltpu.SMEM)]
        + [pl.BlockSpec(memory_space=pl.ANY)] * len(pieces),
        out_specs=pl.BlockSpec(memory_space=pltpu.VMEM),
        scratch_shapes=[pltpu.SemaphoreType.DMA((len(pieces),))],
        cost_estimate=pl.CostEstimate(flops=0, transcendentals=0, bytes_accessed=4 * rows * cols),
    )(offs, *pieces)


def fetch_weight(piece, mx, g):
    rows, cols = piece.shape
    half = rows // 2
    mine, other = g * half, (1 - g) * half
    own_half = lax.dynamic_slice(piece, (mine, 0), (half, cols))
    x_g = swap(own_half, "mx", 2)
    z_g = swap(own_half, "my", 2)
    x_o = swap(x_g, "group", 1)
    z_o = swap(z_g, "group", 1)
    d_g = swap(z_g, "mx", 2)
    d_o = swap(d_g, "group", 1)
    c_own = swap(piece, "mx", 1)
    near = [(piece, mx * rows), (c_own, (mx ^ 1) * rows)]
    far = []
    for part, block, off, to in (
        (x_g, 2, mine, near),
        (x_o, 2, other, near),
        (z_g, 0, mine, far),
        (z_o, 0, other, far),
        (d_g, 2, mine, far),
        (d_o, 2, other, far),
    ):
        to.append((part, (mx ^ block) * rows + off))
        to.append((swap(part, "mx", 1), (mx ^ block ^ 1) * rows + off))
    return tuple(assemble([p for p, _ in grp], [o for _, o in grp]) for grp in (near, far))


def pair_shards(teacher_feats, t_gain, t_bias, projection, student_in, s_gain, w_in, w_out):
    mx = lax.axis_index("mx")
    g = lax.axis_index("group")
    patch_all, image_loc, feat_loc = teacher_feats.shape
    patch_loc = patch_all // 4
    toks = patch_loc * image_loc
    tokens = PATCHES * image_loc * 4

    student_f32 = student_in.reshape(toks, DS).astype(F32)
    student_mean = jnp.sum(student_f32, axis=1, keepdims=True) / DS
    student_square = jnp.sum(student_f32 * student_f32, axis=1, keepdims=True) / DS
    normed_own = (
        (student_f32 - student_mean)
        * lax.rsqrt(student_square - student_mean * student_mean + epsilon)
        * s_gain
    ).astype(BF16)
    normed = jnp.concatenate([normed_own, swap(normed_own, "my", 1)], axis=0)

    in_near, in_far = fetch_weight(w_in, mx, g)
    out_near, out_far = fetch_weight(w_out.T, mx, g)

    features = teacher_feats.astype(F32)
    stats = jnp.stack([jnp.sum(features, axis=2), jnp.sum(features * features, axis=2)])
    stats = stats + swap(stats, "mx", 1)
    stats = stats + swap(stats, "mx", 2)
    row_mean = stats[0] / DT
    rstd = lax.rsqrt(stats[1] / DT - row_mean * row_mean + epsilon)

    def target_part(block):
        start = (mx ^ block) * patch_loc
        feats = lax.dynamic_slice_in_dim(teacher_feats, start, patch_loc, 0).astype(F32)
        mean = lax.dynamic_slice_in_dim(row_mean, start, patch_loc, 0)
        scale = lax.dynamic_slice_in_dim(rstd, start, patch_loc, 0)
        tnorm = (
            (feats - mean[..., None]) * scale[..., None] * t_gain.astype(F32) + t_bias.astype(F32)
        ).astype(BF16)
        return jnp.dot(
            tnorm.reshape(toks, feat_loc), projection, preferred_element_type=F32
        ).astype(BF16)

    q3 = target_part(3)
    q1 = target_part(1)
    q2 = target_part(2)
    q0 = target_part(0)
    t2 = (q2.astype(F32) + swap(q3, "mx", 1).astype(F32)).astype(BF16)
    t0 = q0.astype(F32) + swap(q1, "mx", 1).astype(F32)
    target = t0 + swap(t2, "mx", 2).astype(F32)

    def forward(weight):
        preact = jnp.dot(normed, weight, preferred_element_type=F32)
        return gelu_value(preact).astype(BF16), gelu_slope(preact)

    act_near, slope_near = forward(in_near)
    act_far, slope_far = forward(in_far)

    def nt(left, right):
        return lax.dot_general(left, right, (((1,), (1,)), ((), ())), preferred_element_type=F32)

    branch_pair = (nt(act_near[toks:], out_near) + nt(act_far[toks:], out_far)).astype(BF16)
    branch_recv = swap(branch_pair, "my", 1)
    branch_own = (nt(act_near[:toks], out_near) + nt(act_far[:toks], out_far)).astype(BF16)

    residue = student_f32 + (branch_own.astype(F32) + branch_recv.astype(F32)) - target
    grad_own = (residue / jnp.sqrt(jnp.float32(tokens))).astype(BF16)
    grad = jnp.concatenate([grad_own, swap(grad_own, "my", 1)], axis=0)
    loss = jnp.broadcast_to(jnp.sum(residue * residue), (8, 128))
    for axis, bit in (("my", 1), ("my", 2), ("mx", 1), ("mx", 2)):
        loss = loss + swap(loss, axis, bit)
    mse_loss = loss[0, :1] / (tokens * DS)

    def tn(left, right):
        return lax.dot_general(
            left, right, (((0,), (0,)), ((), ())), preferred_element_type=F32
        ).astype(BF16)

    def reduce_mx(part):
        rows = part.shape[0] // 4
        blocks = [
            lax.dynamic_slice_in_dim(part, (mx ^ k) * rows, rows, 0) for k in range(4)
        ]
        s2 = (blocks[2].astype(F32) + swap(blocks[3], "mx", 1).astype(F32)).astype(BF16)
        s0 = blocks[0].astype(F32) + swap(blocks[1], "mx", 1).astype(F32)
        return s0 + swap(s2, "mx", 2).astype(F32)

    def backward(weight_out, slope, act):
        part_out = tn(grad, act)
        grad_act = jnp.dot(grad, weight_out, preferred_element_type=F32)
        grad_pre = (grad_act * slope).astype(BF16)
        part_in = tn(normed, grad_pre)
        return reduce_mx(part_out), reduce_mx(part_in)

    far_out, far_in = backward(out_far, slope_far, act_far)
    far_out = swap(far_out.astype(BF16), "my", 2)
    far_in = swap(far_in.astype(BF16), "my", 2)
    near_out, near_in = backward(out_near, slope_near, act_near)
    grad_in = near_in + far_in.astype(F32)
    grad_out = (near_out + far_out.astype(F32)).T
    return (mse_loss, grad_in, grad_out)


def shards(teacher_feats, t_gain, t_bias, projection, student_in, s_gain, w_in, w_out):
    patch_all, image_loc, feat_loc = teacher_feats.shape
    mx_count = lax.axis_size("mx")
    my_count = lax.axis_size("my")
    patch_loc = patch_all // mx_count
    features = teacher_feats.astype(jnp.float32)
    feature_sum, squares = lax.psum(
        (jnp.sum(features, axis=2), jnp.sum(features * features, axis=2)), "mx"
    )
    row_mean = feature_sum / DT
    variance = squares / DT - row_mean * row_mean
    normed_teacher = (
        (features - row_mean[..., None])
        * lax.rsqrt(variance + epsilon)[..., None]
        * t_gain.astype(jnp.float32)
        + t_bias.astype(jnp.float32)
    ).astype(jnp.bfloat16)
    flattened = normed_teacher.reshape(patch_loc * lax.axis_size("mx") * image_loc, feat_loc)
    target = lax.psum_scatter(
        jnp.dot(flattened, projection, preferred_element_type=jnp.float32)
        .reshape(patch_loc * lax.axis_size("mx"), image_loc, DS)
        .astype(jnp.bfloat16),
        "mx",
        scatter_dimension=0,
        tiled=True,
    ).astype(jnp.float32)
    student_f32 = student_in.astype(jnp.float32)
    student_mean = jnp.sum(student_f32, axis=2, keepdims=True) / DS
    student_square = jnp.sum(student_f32 * student_f32, axis=2, keepdims=True) / DS
    normed = (
        (student_f32 - student_mean)
        * lax.rsqrt(student_square - student_mean * student_mean + epsilon)
        * s_gain
    ).astype(jnp.bfloat16)
    gathered = lax.all_gather(normed, "my", axis=1, tiled=True)
    rows_all = patch_loc * image_loc * my_count
    normed_flat = gathered.reshape(rows_all, DS)
    preact = jnp.dot(
        normed_flat,
        lax.all_gather(w_in, "mx", axis=0, tiled=True),
        preferred_element_type=jnp.float32,
    )
    activation = gelu_value(preact).astype(jnp.bfloat16)
    w_out_full = lax.all_gather(w_out, "mx", axis=1, tiled=True)
    branch_part = jnp.dot(activation, w_out_full, preferred_element_type=jnp.float32).reshape(
        patch_loc, image_loc * my_count, DS
    )
    branch = lax.psum_scatter(
        branch_part.astype(jnp.bfloat16), "my", scatter_dimension=1, tiled=True
    ).astype(jnp.float32)
    residue = student_f32 + branch - target
    tokens = PATCHES * image_loc * my_count
    squared_sum = lax.psum(jnp.sum(residue * residue), ("mx", "my"))
    mse_loss = jnp.reshape(squared_sum / (tokens * DS), (1,))
    grad_output = (residue / jnp.sqrt(jnp.float32(tokens))).astype(jnp.bfloat16)
    grad_rows = lax.all_gather(grad_output, "my", axis=1, tiled=True).reshape(rows_all, DS)
    grad_act = lax.dot_general(
        grad_rows, w_out_full, (((1,), (1,)), ((), ())), preferred_element_type=jnp.float32
    )
    grad_pre = (grad_act * gelu_slope(preact)).astype(jnp.bfloat16)
    part_in = lax.dot_general(
        normed_flat, grad_pre, (((0,), (0,)), ((), ())), preferred_element_type=jnp.float32
    )
    part_out = lax.dot_general(
        activation, grad_rows, (((0,), (0,)), ((), ())), preferred_element_type=jnp.float32
    )
    grad_in = lax.psum_scatter(
        part_in.astype(jnp.bfloat16), "mx", scatter_dimension=0, tiled=True
    ).astype(jnp.float32)
    grad_out = lax.psum_scatter(
        part_out.astype(jnp.bfloat16), "mx", scatter_dimension=1, tiled=True
    ).astype(jnp.float32)
    return (mse_loss, grad_in, grad_out)


def solution(mesh):
    in_specs = (
        P(None, ("group", "my"), "mx"),
        P("mx"),
        P("mx"),
        P("mx", None),
        P("mx", ("group", "my"), None),
        P(),
        P("mx", "my"),
        P("my", "mx"),
    )
    out_specs = (P("group"), P(("group", "mx"), "my"), P(("group", "my"), "mx"))
    pairs = mesh.shape["group"] == 2 and mesh.shape["mx"] == 4 and mesh.shape["my"] == 4
    body = pair_shards if pairs else shards
    return jax.shard_map(body, mesh=mesh, in_specs=in_specs, out_specs=out_specs, check_vma=False)
```

```python
import jax
import jax.numpy as jnp
from jax import lax
from jax.experimental import pallas as pl
from jax.experimental.pallas import tpu as pltpu
from jax.sharding import PartitionSpec as P

DT = 6144
DS = 1408
PATCHES = 256
F32 = jnp.float32
BF16 = jnp.bfloat16

epsilon = 1e-06

FC = 256
TINY = pl.CostEstimate(flops=1000, transcendentals=0, bytes_accessed=1000)
PARAMS = pltpu.CompilerParams(vmem_limit_bytes=58 * 2**20)
LIGHT = pltpu.CompilerParams(vmem_limit_bytes=24 * 2**20)


def gelu_value(value):
    return 0.5 * value * (1.0 + lax.erf(value * 0.7071067811865476))


def gelu_slope(value):
    return (
        0.5 * (1.0 + lax.erf(value * 0.7071067811865476))
        + value * jnp.exp(-0.5 * value * value) * 0.3989422804014327
    )


def swap(value, axis, bit):
    count = lax.axis_size(axis)
    return lax.ppermute(value, axis, [(i, i ^ bit) for i in range(count)])


def assemble(pieces, rows):
    arrays = [p[0] for p in pieces]
    cols = arrays[0].shape[1]
    offs = jnp.stack([jnp.asarray(p[3], jnp.int32) for p in pieces])

    def body(offs_ref, *refs):
        parts, out, sems = refs[:-2], refs[-2], refs[-1]
        copies = []
        for i, part in enumerate(parts):
            first, count = pieces[i][1:3]
            off = pl.multiple_of(offs_ref[i], 16)
            copies.append(
                pltpu.make_async_copy(
                    part.at[first : first + count, :], out.at[pl.ds(off, count), :], sems.at[i]
                )
            )
        for copy in copies:
            copy.start()
        for copy in copies:
            copy.wait()

    return pl.pallas_call(
        body,
        out_shape=jax.ShapeDtypeStruct((rows, cols), arrays[0].dtype),
        in_specs=[pl.BlockSpec(memory_space=pltpu.SMEM)]
        + [pl.BlockSpec(memory_space=pl.ANY)] * len(pieces),
        out_specs=pl.BlockSpec(memory_space=pltpu.VMEM),
        scratch_shapes=[pltpu.SemaphoreType.DMA((len(pieces),))],
        cost_estimate=TINY,
        compiler_params=PARAMS,
        name="assemble",
    )(offs, *arrays)


def whole(shape):
    return pl.BlockSpec(shape, lambda j: (0,) * len(shape))


def turned(value):
    part = value[:, :128]
    for at in range(128, value.shape[1], 128):
        part = part + value[:, at : at + 128]
    return jnp.sum(part.T, axis=0, keepdims=True)


def teacher_sums(feats):
    count, width = feats.shape
    step = 512

    def body(x_ref, out):
        x = x_ref[...].astype(F32)
        out[0:1, :] = turned(x)
        out[1:2, :] = turned(x * x)
        out[2:, :] = jnp.zeros((6, step), F32)

    return pl.pallas_call(
        body,
        grid=(count // step,),
        in_specs=[pl.BlockSpec((step, width), lambda j: (j, 0))],
        out_specs=pl.BlockSpec((8, step), lambda j: (0, j)),
        out_shape=jax.ShapeDtypeStruct((8, count), F32),
        compiler_params=PARAMS,
        cost_estimate=TINY,
        name="teacher_sums",
    )(feats)


def target_parts(mx, ks, feats, sums, gain, bias, projection):
    count, width = feats.shape
    step = 256
    toks = count // 4
    per = toks // step

    def body(mx_ref, x_ref, s_ref, g_ref, b_ref, w_ref, *outs):
        j = pl.program_id(0)
        sums_t = jnp.concatenate([s_ref[...], jnp.zeros((6, step), F32)], axis=0).T
        mean = sums_t[:, 0:1] / DT
        rstd = lax.rsqrt(sums_t[:, 1:2] / DT - mean * mean + epsilon)
        tnorm = (x_ref[...].astype(F32) - mean) * rstd * g_ref[...] + b_ref[...]
        value = jnp.dot(tnorm.astype(BF16), w_ref[...], preferred_element_type=F32).astype(BF16)
        for n, out in enumerate(outs):

            @pl.when(j // per == n)
            def _(out=out):
                out[...] = value

    def row(j, mx_ref):
        k = ks[0] - j // per
        return (mx_ref[0] ^ k) * per + j % per

    return pl.pallas_call(
        body,
        grid_spec=pltpu.PrefetchScalarGridSpec(
            num_scalar_prefetch=1,
            grid=(len(ks) * per,),
            in_specs=[
                pl.BlockSpec((step, width), lambda j, m: (row(j, m), 0)),
                pl.BlockSpec((2, step), lambda j, m: (0, row(j, m))),
                pl.BlockSpec((1, width), lambda j, m: (0, 0)),
                pl.BlockSpec((1, width), lambda j, m: (0, 0)),
                pl.BlockSpec((width, DS), lambda j, m: (0, 0)),
            ],
            out_specs=[
                pl.BlockSpec(
                    (step, DS), lambda j, m, n=n: (jnp.clip(j - n * per, 0, per - 1), 0)
                )
                for n in range(len(ks))
            ],
        ),
        out_shape=[jax.ShapeDtypeStruct((toks, DS), BF16)] * len(ks),
        compiler_params=PARAMS,
        cost_estimate=TINY,
        name="targets",
    )(mx, feats, sums, gain, bias, projection)


def student_norm(student, gain):
    count, width = student.shape
    step = 128

    def body(x_ref, g_ref, out):
        x = x_ref[...].astype(F32)
        mean = jnp.sum(x, axis=1, keepdims=True) / DS
        square = jnp.sum(x * x, axis=1, keepdims=True) / DS
        out[...] = ((x - mean) * lax.rsqrt(square - mean * mean + epsilon) * g_ref[...]).astype(BF16)

    return pl.pallas_call(
        body,
        grid=(count // step,),
        in_specs=[
            pl.BlockSpec((step, width), lambda j: (j, 0)),
            pl.BlockSpec((1, width), lambda j: (0, 0)),
        ],
        out_specs=pl.BlockSpec((step, width), lambda j: (j, 0)),
        out_shape=jax.ShapeDtypeStruct((count, width), BF16),
        compiler_params=PARAMS,
        cost_estimate=TINY,
        name="student_norm",
    )(student, gain)


def forward_part(normed_own, normed_pair, weight):
    toks = normed_own.shape[0]
    cols = weight.shape[1]

    def body(no, np_, w, pre, act):
        for part, off in ((no, 0), (np_, toks)):
            value = jnp.dot(part[...], w[...], preferred_element_type=F32)
            pre[off : off + toks, :] = value
            act[off : off + toks, :] = gelu_value(value).astype(BF16)

    chunk = pl.BlockSpec((2 * toks, FC), lambda j: (0, j))
    return pl.pallas_call(
        body,
        grid=(cols // FC,),
        in_specs=[whole((toks, DS)), whole((toks, DS)), pl.BlockSpec((DS, FC), lambda j: (0, j))],
        out_specs=[chunk, chunk],
        out_shape=[
            jax.ShapeDtypeStruct((2 * toks, cols), F32),
            jax.ShapeDtypeStruct((2 * toks, cols), BF16),
        ],
        compiler_params=PARAMS,
        cost_estimate=TINY,
        name="forward",
    )(normed_own, normed_pair, weight)


def branch_part(act_near, act_far, w_near, w_far, which, dtype):
    toks = act_near.shape[0] // 2
    cols = act_near.shape[1]
    step = 2 * FC
    n = cols // step

    def body(an, af, wn, wf, out, acc):
        j = pl.program_id(0)

        @pl.when(j == 0)
        def _():
            acc[...] = jnp.zeros_like(acc)

        @pl.when(j < n)
        def _():
            acc[...] += nt(an[...], wn[...])

        @pl.when(j >= n)
        def _():
            acc[...] += nt(af[...], wf[...])

        @pl.when(j == 2 * n - 1)
        def _():
            out[...] = acc[...].astype(out.dtype)

    near = lambda j: jnp.minimum(j, n - 1)
    far = lambda j: jnp.maximum(j - n, 0)
    return pl.pallas_call(
        body,
        grid=(2 * n,),
        in_specs=[
            pl.BlockSpec((toks, step), lambda j: (which, near(j))),
            pl.BlockSpec((toks, step), lambda j: (which, far(j))),
            pl.BlockSpec((DS, step), lambda j: (0, near(j))),
            pl.BlockSpec((DS, step), lambda j: (0, far(j))),
        ],
        out_specs=whole((toks, DS)),
        out_shape=jax.ShapeDtypeStruct((toks, DS), dtype),
        scratch_shapes=[pltpu.VMEM((toks, DS), F32)],
        compiler_params=PARAMS,
        cost_estimate=TINY,
        name="branch",
    )(act_near, act_far, w_near, w_far)


def store_blocks(mx, acc, scratch, outs):
    if len(outs) == 1:
        outs[0][...] = acc.astype(BF16)
        return
    rows = DS // 4
    scratch[...] = acc.astype(BF16)
    for k, out in enumerate(outs):
        off = pl.multiple_of((mx ^ k) * rows, 32)
        out[...] = scratch[pl.ds(off, rows), :]


def block_outs(split, cols):
    count, rows = (4, DS // 4) if split else (1, DS)
    specs = [pl.BlockSpec((rows, FC), lambda j: (0, j))] * count
    shapes = [jax.ShapeDtypeStruct((rows, cols), BF16)] * count
    return specs, shapes


def grad_out_part(mx, grad_own, grad_pair, act, split):
    toks = grad_own.shape[0]
    cols = act.shape[1]
    specs, shapes = block_outs(split, cols)

    def body(mx_ref, go, gp, a, *rest):
        outs, (gt, scratch) = rest[:-2], rest[-2:]

        @pl.when(pl.program_id(0) == 0)
        def _():
            gt[:, :toks] = go[...].T
            gt[:, toks:] = gp[...].T

        acc = jnp.dot(gt[...], a[...], preferred_element_type=F32)
        store_blocks(mx_ref[0], acc, scratch, outs)

    return pl.pallas_call(
        body,
        grid=(cols // FC,),
        in_specs=[
            pl.BlockSpec(memory_space=pltpu.SMEM),
            whole((toks, DS)),
            whole((toks, DS)),
            pl.BlockSpec((2 * toks, FC), lambda j: (0, j)),
        ],
        out_specs=specs,
        out_shape=shapes,
        scratch_shapes=[pltpu.VMEM((DS, 2 * toks), BF16), pltpu.VMEM((DS, FC), BF16)],
        compiler_params=LIGHT,
        cost_estimate=TINY,
        name="grad_out",
    )(mx, grad_own, grad_pair, act)


def grad_in_part(mx, grad_own, grad_pair, w_out, slope, normed_t, split):
    toks = grad_own.shape[0]
    cols = w_out.shape[1]
    specs, shapes = block_outs(split, cols)

    def body(mx_ref, go, gp, w, sl, nrm, *rest):
        outs, (pre, scratch) = rest[:-2], rest[-2:]
        for part, off in ((go, 0), (gp, toks)):
            act_grad = jnp.dot(part[...], w[...], preferred_element_type=F32)
            pre[off : off + toks, :] = (act_grad * sl[off : off + toks, :]).astype(BF16)
        acc = jnp.dot(nrm[...], pre[...], preferred_element_type=F32)
        store_blocks(mx_ref[0], acc, scratch, outs)

    return pl.pallas_call(
        body,
        grid=(cols // FC,),
        in_specs=[
            pl.BlockSpec(memory_space=pltpu.SMEM),
            whole((toks, DS)),
            whole((toks, DS)),
            pl.BlockSpec((DS, FC), lambda j: (0, j)),
            pl.BlockSpec((2 * toks, FC), lambda j: (0, j)),
            whole((DS, 2 * toks)),
        ],
        out_specs=specs,
        out_shape=shapes,
        scratch_shapes=[pltpu.VMEM((2 * toks, FC), BF16), pltpu.VMEM((DS, FC), BF16)],
        compiler_params=LIGHT,
        cost_estimate=TINY,
        name="grad_in",
    )(mx, grad_own, grad_pair, w_out, slope, normed_t)


def after(value, *deps):
    return lax.optimization_barrier((value,) + deps)[0]


def together(*values):
    return lax.optimization_barrier(values)


def nt(left, right):
    return lax.dot_general(left, right, (((1,), (1,)), ((), ())), preferred_element_type=F32)


def tn(left, right):
    return lax.dot_general(
        left, right, (((0,), (0,)), ((), ())), preferred_element_type=F32
    ).astype(BF16)


def pair_shards(teacher_feats, t_gain, t_bias, projection, student_in, s_gain, w_in, w_out):
    mx = lax.axis_index("mx")
    g = lax.axis_index("group")
    patch_all, image_loc, feat_loc = teacher_feats.shape
    patch_loc = patch_all // 4
    toks = patch_loc * image_loc
    tokens = PATCHES * image_loc * 4
    w_out = w_out.T
    rows, cols = w_in.shape
    half = rows // 2
    mine, other = g * half, (1 - g) * half

    mx1 = mx.reshape(1).astype(jnp.int32)

    def my_half(w):
        return lax.dynamic_slice(w, (mine, 0), (half, cols))

    z_send = jnp.concatenate([my_half(w_in), my_half(w_out)], axis=0)
    z_g = swap(z_send, "my", 2)
    in_near = lax.all_gather(w_in, "mx", axis=0, tiled=True)
    out_near = lax.all_gather(w_out, "mx", axis=0, tiled=True)

    feats = teacher_feats.reshape(4 * toks, feat_loc)
    student = student_in.reshape(toks, DS)
    normed_own = student_norm(after(student, z_send), s_gain.reshape(1, DS))
    normed_pair = swap(normed_own, "my", 1)
    sums = teacher_sums(after(feats, normed_own))
    sums = lax.psum(sums[:2], "mx")
    gain = t_gain.astype(F32).reshape(1, feat_loc)
    bias = t_bias.astype(F32).reshape(1, feat_loc)
    parts = target_parts(mx1, (3, 2, 1, 0), feats, sums, gain, bias, projection)
    q3, q2, q1, q0, z_g, normed_pair = together(*parts, z_g, normed_pair)

    d_g = swap(z_g, "mx", 2)
    z_o = swap(z_g, "group", 1)
    zgc = swap(z_g, "mx", 1)
    q3c = swap(q3, "mx", 1)
    pre_near, act_near = forward_part(normed_own, normed_pair, in_near)
    pre_near, act_near, d_g, z_o, zgc, q3c = together(pre_near, act_near, d_g, z_o, zgc, q3c)
    in_do = swap(d_g[:half], "group", 1)
    out_do = swap(z_o[half:], "mx", 2)
    zoc, dgc = swap(z_o, "mx", 1), swap(d_g, "mx", 1)
    in_do, out_do, zoc, dgc = together(in_do, out_do, zoc, dgc)
    in_doc, out_doc = swap(in_do, "mx", 1), swap(out_do, "mx", 1)
    t2 = (q2.astype(F32) + q3c.astype(F32)).astype(BF16)
    in_doc, out_doc, t2 = together(in_doc, out_doc, t2)

    def far_rows(first, d_o, d_oc):
        out = []
        for part, part_c, block, off, at in (
            (z_g, zgc, 0, mine, first),
            (z_o, zoc, 0, other, first),
            (d_g, dgc, 2, mine, first),
            (d_o, d_oc, 2, other, 0),
        ):
            out.append((part, at, half, (mx ^ block) * rows + off))
            out.append((part_c, at, half, (mx ^ block ^ 1) * rows + off))
        return out

    in_far = assemble(far_rows(0, in_do, in_doc), DS)
    target_x = swap(t2, "mx", 2)
    q1c = swap(after(q1, in_doc), "mx", 1)
    pre_far, act_far = forward_part(normed_own, normed_pair, in_far)
    pre_far, act_far, q1c, out_doc = together(pre_far, act_far, q1c, out_doc)
    out_far = assemble(far_rows(half, out_do, out_doc), DS)
    t0 = q0.astype(F32) + q1c.astype(F32)

    branch_pair = branch_part(act_near, act_far, out_near, out_far, 1, BF16)
    branch_recv = swap(branch_pair, "my", 1)
    branch_own = branch_part(after(act_near, branch_pair), act_far, out_near, out_far, 0, F32)
    slope_far = gelu_slope(after(pre_far, branch_own))
    slope_near = gelu_slope(after(pre_near, slope_far))
    normed_t = jnp.concatenate([after(normed_own, slope_near).T, normed_pair.T], axis=1)
    branch_recv = after(branch_recv, normed_t)

    target = t0 + target_x.astype(F32)
    residue = student.astype(F32) + (branch_own + branch_recv.astype(F32)) - target
    grad_own = (residue / jnp.sqrt(jnp.float32(tokens))).astype(BF16)
    loss = jnp.broadcast_to(jnp.sum(residue * residue), (8, 128))
    grad_own, loss = lax.optimization_barrier((grad_own, loss))
    grad_pair = swap(grad_own, "my", 1)
    for bit in (1, 2):
        loss = loss + swap(loss, "mx", bit)
    grad_pair = after(grad_pair, loss)

    loss_z = swap(loss, "my", 1)
    o0, o1, o2, o3 = grad_out_part(mx1, grad_own, grad_pair, act_far, True)
    o0, o1, o2, o3, loss_z = together(o0, o1, o2, o3, loss_z)
    loss = loss + loss_z
    loss_z = swap(loss, "my", 2)
    got2, got0 = swap(o3, "mx", 1), swap(o1, "mx", 1)
    h0, h1 = slice(0, half), slice(half, rows)
    s2_out = [(o2[c].astype(F32) + got2[c].astype(F32)).astype(BF16) for c in (h0, h1)]
    x_out = [swap(v, "mx", 2) for v in s2_out]
    i0, i1, i2, i3 = grad_in_part(
        mx1, after(grad_own, *s2_out), grad_pair, out_far, slope_far, normed_t, True
    )
    i0, i1, i2, i3, x_out0, got0, loss_z = together(i0, i1, i2, i3, x_out[0], got0, loss_z)
    mse_loss = (loss + loss_z)[0, :1] / (tokens * DS)

    def last(keep, got, x):
        return (keep.astype(F32) + got.astype(F32) + x.astype(F32)).astype(BF16)

    f0 = last(o0[h0], got0[h0], x_out0)
    f_out0 = swap(f0, "my", 2)
    gin2, gin0 = swap(after(i3, f0), "mx", 1), swap(after(i1, f0), "mx", 1)
    s2_in = (i2.astype(F32) + gin2.astype(F32)).astype(BF16)
    x_in = swap(s2_in, "mx", 2)
    n0, n1, n2, n3 = grad_out_part(mx1, after(grad_own, s2_in), grad_pair, act_near, True)
    n0, n1, n2, n3, x_out1, gin0, f_out0 = together(n0, n1, n2, n3, x_out[1], gin0, f_out0)
    f1 = last(o0[h1], got0[h1], x_out1)
    f_out1 = swap(f1, "my", 2)
    gn2, gn0 = swap(after(n3, f1), "mx", 1), swap(after(n1, f1), "mx", 1)
    gn2, gn0 = together(gn2, gn0)
    s2_on = (n2.astype(F32) + gn2.astype(F32)).astype(BF16)
    x_on = swap(s2_on, "mx", 2)
    m0, m1, m2, m3 = grad_in_part(
        mx1, after(grad_own, s2_on), grad_pair, out_near, slope_near, normed_t, True
    )
    m0, m1, m2, m3, x_in, f_out1 = together(m0, m1, m2, m3, x_in, f_out1)
    f2 = [last(i0[c], gin0[c], x_in[c]) for c in (h0, h1)]
    f_in = [swap(v, "my", 2) for v in f2]
    gm2, gm0 = swap(after(m3, *f2), "mx", 1), swap(after(m1, *f2), "mx", 1)
    gm2, gm0, x_on, f_in0 = together(gm2, gm0, x_on, f_in[0])
    s2_mn = (m2.astype(F32) + gm2.astype(F32)).astype(BF16)
    x_mn = swap(s2_mn, "mx", 2)
    grad_out_near = n0.astype(F32) + gn0.astype(F32) + x_on.astype(F32)
    grad_in_near = m0.astype(F32) + gm0.astype(F32) + x_mn.astype(F32)
    f_out = jnp.concatenate([f_out0, f_out1], axis=0)
    f_in = jnp.concatenate([f_in0, f_in[1]], axis=0)
    grad_out = (grad_out_near + f_out.astype(F32)).T
    grad_in = grad_in_near + f_in.astype(F32)
    return (mse_loss, grad_in, grad_out)


def shards(teacher_feats, t_gain, t_bias, projection, student_in, s_gain, w_in, w_out):
    patch_all, image_loc, feat_loc = teacher_feats.shape
    mx_count = lax.axis_size("mx")
    my_count = lax.axis_size("my")
    patch_loc = patch_all // mx_count
    features = teacher_feats.astype(jnp.float32)
    feature_sum, squares = lax.psum(
        (jnp.sum(features, axis=2), jnp.sum(features * features, axis=2)), "mx"
    )
    row_mean = feature_sum / DT
    variance = squares / DT - row_mean * row_mean
    normed_teacher = (
        (features - row_mean[..., None])
        * lax.rsqrt(variance + epsilon)[..., None]
        * t_gain.astype(jnp.float32)
        + t_bias.astype(jnp.float32)
    ).astype(jnp.bfloat16)
    flattened = normed_teacher.reshape(patch_loc * lax.axis_size("mx") * image_loc, feat_loc)
    target = lax.psum_scatter(
        jnp.dot(flattened, projection, preferred_element_type=jnp.float32)
        .reshape(patch_loc * lax.axis_size("mx"), image_loc, DS)
        .astype(jnp.bfloat16),
        "mx",
        scatter_dimension=0,
        tiled=True,
    ).astype(jnp.float32)
    student_f32 = student_in.astype(jnp.float32)
    student_mean = jnp.sum(student_f32, axis=2, keepdims=True) / DS
    student_square = jnp.sum(student_f32 * student_f32, axis=2, keepdims=True) / DS
    normed = (
        (student_f32 - student_mean)
        * lax.rsqrt(student_square - student_mean * student_mean + epsilon)
        * s_gain
    ).astype(jnp.bfloat16)
    gathered = lax.all_gather(normed, "my", axis=1, tiled=True)
    rows_all = patch_loc * image_loc * my_count
    normed_flat = gathered.reshape(rows_all, DS)
    preact = jnp.dot(
        normed_flat,
        lax.all_gather(w_in, "mx", axis=0, tiled=True),
        preferred_element_type=jnp.float32,
    )
    activation = gelu_value(preact).astype(jnp.bfloat16)
    w_out_full = lax.all_gather(w_out, "mx", axis=1, tiled=True)
    branch_part = jnp.dot(activation, w_out_full, preferred_element_type=jnp.float32).reshape(
        patch_loc, image_loc * my_count, DS
    )
    branch = lax.psum_scatter(
        branch_part.astype(jnp.bfloat16), "my", scatter_dimension=1, tiled=True
    ).astype(jnp.float32)
    residue = student_f32 + branch - target
    tokens = PATCHES * image_loc * my_count
    squared_sum = lax.psum(jnp.sum(residue * residue), ("mx", "my"))
    mse_loss = jnp.reshape(squared_sum / (tokens * DS), (1,))
    grad_output = (residue / jnp.sqrt(jnp.float32(tokens))).astype(jnp.bfloat16)
    grad_rows = lax.all_gather(grad_output, "my", axis=1, tiled=True).reshape(rows_all, DS)
    grad_act = lax.dot_general(
        grad_rows, w_out_full, (((1,), (1,)), ((), ())), preferred_element_type=jnp.float32
    )
    grad_pre = (grad_act * gelu_slope(preact)).astype(jnp.bfloat16)
    part_in = lax.dot_general(
        normed_flat, grad_pre, (((0,), (0,)), ((), ())), preferred_element_type=jnp.float32
    )
    part_out = lax.dot_general(
        activation, grad_rows, (((0,), (0,)), ((), ())), preferred_element_type=jnp.float32
    )
    grad_in = lax.psum_scatter(
        part_in.astype(jnp.bfloat16), "mx", scatter_dimension=0, tiled=True
    ).astype(jnp.float32)
    grad_out = lax.psum_scatter(
        part_out.astype(jnp.bfloat16), "mx", scatter_dimension=1, tiled=True
    ).astype(jnp.float32)
    return (mse_loss, grad_in, grad_out)


def solution(mesh):
    in_specs = (
        P(None, ("group", "my"), "mx"),
        P("mx"),
        P("mx"),
        P("mx", None),
        P("mx", ("group", "my"), None),
        P(),
        P("mx", "my"),
        P("my", "mx"),
    )
    out_specs = (P("group"), P(("group", "mx"), "my"), P(("group", "my"), "mx"))
    pairs = mesh.shape["group"] == 2 and mesh.shape["mx"] == 4 and mesh.shape["my"] == 4
    body = pair_shards if pairs else shards
    return jax.shard_map(body, mesh=mesh, in_specs=in_specs, out_specs=out_specs, check_vma=False)
```

```python
import jax
import jax.numpy as jnp
from jax import lax
from jax.experimental import pallas as pl
from jax.experimental.pallas import tpu as pltpu
from jax.sharding import PartitionSpec as P

DT = 6144
DS = 1408
PATCHES = 256
F32 = jnp.float32
BF16 = jnp.bfloat16

epsilon = 1e-06

FC = 256
TINY = pl.CostEstimate(flops=1000, transcendentals=0, bytes_accessed=1000)
PARAMS = pltpu.CompilerParams(vmem_limit_bytes=58 * 2**20)
LIGHT = pltpu.CompilerParams(vmem_limit_bytes=24 * 2**20)


def gelu_value(value):
    return 0.5 * value * (1.0 + lax.erf(value * 0.7071067811865476))


def gelu_slope(value):
    return (
        0.5 * (1.0 + lax.erf(value * 0.7071067811865476))
        + value * jnp.exp(-0.5 * value * value) * 0.3989422804014327
    )


def swap(value, axis, bit):
    count = lax.axis_size(axis)
    return lax.ppermute(value, axis, [(i, i ^ bit) for i in range(count)])


def piece_copies(pieces, offs_ref, parts, out, sems):
    copies = []
    for i, part in enumerate(parts):
        first, count = pieces[i][1:3]
        off = pl.multiple_of(offs_ref[i], 16)
        copies.append(
            pltpu.make_async_copy(
                part.at[first : first + count, :], out.at[pl.ds(off, count), :], sems.at[i]
            )
        )
    return copies


def piece_offsets(pieces):
    return jnp.stack([jnp.asarray(p[3], jnp.int32) for p in pieces])


def assemble(pieces, rows):
    arrays = [p[0] for p in pieces]
    cols = arrays[0].shape[1]
    offs = piece_offsets(pieces)

    def body(offs_ref, *refs):
        parts, out, sems = refs[:-2], refs[-2], refs[-1]
        copies = piece_copies(pieces, offs_ref, parts, out, sems)
        for copy in copies:
            copy.start()
        for copy in copies:
            copy.wait()

    return pl.pallas_call(
        body,
        out_shape=jax.ShapeDtypeStruct((rows, cols), arrays[0].dtype),
        in_specs=[pl.BlockSpec(memory_space=pltpu.SMEM)]
        + [pl.BlockSpec(memory_space=pl.ANY)] * len(pieces),
        out_specs=pl.BlockSpec(memory_space=pltpu.VMEM),
        scratch_shapes=[pltpu.SemaphoreType.DMA((len(pieces),))],
        cost_estimate=TINY,
        compiler_params=PARAMS,
        name="assemble",
    )(offs, *arrays)


def whole(shape):
    return pl.BlockSpec(shape, lambda j: (0,) * len(shape))


def turned(value):
    part = value[:, :128]
    for at in range(128, value.shape[1], 128):
        part = part + value[:, at : at + 128]
    return jnp.sum(part.T, axis=0, keepdims=True)


def teacher_sums(feats):
    count, width = feats.shape
    step = 512

    def body(x_ref, out):
        x = x_ref[...].astype(F32)
        out[0:1, :] = turned(x)
        out[1:2, :] = turned(x * x)
        out[2:, :] = jnp.zeros((6, step), F32)

    return pl.pallas_call(
        body,
        grid=(count // step,),
        in_specs=[pl.BlockSpec((step, width), lambda j: (j, 0))],
        out_specs=pl.BlockSpec((8, step), lambda j: (0, j)),
        out_shape=jax.ShapeDtypeStruct((8, count), F32),
        compiler_params=PARAMS,
        cost_estimate=TINY,
        name="teacher_sums",
    )(feats)


def target_parts(mx, ks, feats, sums, gain, bias, projection):
    count, width = feats.shape
    step = 256
    toks = count // 4
    per = toks // step

    def body(mx_ref, x_ref, s_ref, g_ref, b_ref, w_ref, *outs):
        j = pl.program_id(0)
        sums_t = jnp.concatenate([s_ref[...], jnp.zeros((6, step), F32)], axis=0).T
        mean = sums_t[:, 0:1] / DT
        rstd = lax.rsqrt(sums_t[:, 1:2] / DT - mean * mean + epsilon)
        tnorm = (x_ref[...].astype(F32) - mean) * rstd * g_ref[...] + b_ref[...]
        value = jnp.dot(tnorm.astype(BF16), w_ref[...], preferred_element_type=F32).astype(BF16)
        for n, out in enumerate(outs):

            @pl.when(j // per == n)
            def _(out=out):
                out[...] = value

    def row(j, mx_ref):
        k = ks[0] - j // per
        return (mx_ref[0] ^ k) * per + j % per

    return pl.pallas_call(
        body,
        grid_spec=pltpu.PrefetchScalarGridSpec(
            num_scalar_prefetch=1,
            grid=(len(ks) * per,),
            in_specs=[
                pl.BlockSpec((step, width), lambda j, m: (row(j, m), 0)),
                pl.BlockSpec((2, step), lambda j, m: (0, row(j, m))),
                pl.BlockSpec((1, width), lambda j, m: (0, 0)),
                pl.BlockSpec((1, width), lambda j, m: (0, 0)),
                pl.BlockSpec((width, DS), lambda j, m: (0, 0)),
            ],
            out_specs=[
                pl.BlockSpec(
                    (step, DS), lambda j, m, n=n: (jnp.clip(j - n * per, 0, per - 1), 0)
                )
                for n in range(len(ks))
            ],
        ),
        out_shape=[jax.ShapeDtypeStruct((toks, DS), BF16)] * len(ks),
        compiler_params=PARAMS,
        cost_estimate=TINY,
        name="targets",
    )(mx, feats, sums, gain, bias, projection)


def student_norm(student, gain):
    count, width = student.shape
    step = 128

    def body(x_ref, g_ref, out):
        x = x_ref[...].astype(F32)
        mean = jnp.sum(x, axis=1, keepdims=True) / DS
        square = jnp.sum(x * x, axis=1, keepdims=True) / DS
        out[...] = ((x - mean) * lax.rsqrt(square - mean * mean + epsilon) * g_ref[...]).astype(BF16)

    return pl.pallas_call(
        body,
        grid=(count // step,),
        in_specs=[
            pl.BlockSpec((step, width), lambda j: (j, 0)),
            pl.BlockSpec((1, width), lambda j: (0, 0)),
        ],
        out_specs=pl.BlockSpec((step, width), lambda j: (j, 0)),
        out_shape=jax.ShapeDtypeStruct((count, width), BF16),
        compiler_params=LIGHT,
        cost_estimate=TINY,
        name="student_norm",
    )(student, gain)


def forward_part(normed_own, normed_pair, weight):
    toks = normed_own.shape[0]
    cols = weight.shape[1]

    def body(no, np_, w, pre, act):
        for part, off in ((no, 0), (np_, toks)):
            value = jnp.dot(part[...], w[...], preferred_element_type=F32)
            pre[off : off + toks, :] = value
            act[off : off + toks, :] = gelu_value(value).astype(BF16)

    chunk = pl.BlockSpec((2 * toks, FC), lambda j: (0, j))
    return pl.pallas_call(
        body,
        grid=(cols // FC,),
        in_specs=[whole((toks, DS)), whole((toks, DS)), pl.BlockSpec((DS, FC), lambda j: (0, j))],
        out_specs=[chunk, chunk],
        out_shape=[
            jax.ShapeDtypeStruct((2 * toks, cols), F32),
            jax.ShapeDtypeStruct((2 * toks, cols), BF16),
        ],
        compiler_params=PARAMS,
        cost_estimate=TINY,
        name="forward",
    )(normed_own, normed_pair, weight)


def forward_pieces(normed_own, normed_pair, pieces):
    toks = normed_own.shape[0]
    cols = pieces[0][0].shape[1]
    count = len(pieces)

    def body(offs_ref, no, np_, *refs):
        parts, (pre, act, w, sems) = refs[:count], refs[count:]
        j = pl.program_id(0)

        @pl.when(j == 0)
        def _():
            copies = piece_copies(pieces, offs_ref, parts, w, sems)
            for copy in copies:
                copy.start()
            for copy in copies:
                copy.wait()

        chunk = w[:, pl.ds(pl.multiple_of(j * FC, FC), FC)]
        for part, off in ((no, 0), (np_, toks)):
            value = jnp.dot(part[...], chunk, preferred_element_type=F32)
            pre[off : off + toks, :] = value
            act[off : off + toks, :] = gelu_value(value).astype(BF16)

    chunk = pl.BlockSpec((2 * toks, FC), lambda j: (0, j))
    return pl.pallas_call(
        body,
        grid=(cols // FC,),
        in_specs=[pl.BlockSpec(memory_space=pltpu.SMEM), whole((toks, DS)), whole((toks, DS))]
        + [pl.BlockSpec(memory_space=pl.ANY)] * count,
        out_specs=[chunk, chunk],
        out_shape=[
            jax.ShapeDtypeStruct((2 * toks, cols), F32),
            jax.ShapeDtypeStruct((2 * toks, cols), BF16),
        ],
        scratch_shapes=[pltpu.VMEM((DS, cols), BF16), pltpu.SemaphoreType.DMA((count,))],
        compiler_params=PARAMS,
        cost_estimate=TINY,
        name="forward_far",
    )(piece_offsets(pieces), normed_own, normed_pair, *[p[0] for p in pieces])


def branch_pieces(near, act, pieces, which, dtype):
    toks = act.shape[0] // 2
    cols = act.shape[1]
    step = 2 * FC
    n = cols // step
    count = len(pieces)

    def body(offs_ref, nr, a, *refs):
        parts, (out, acc, w, sems) = refs[:count], refs[count:]
        j = pl.program_id(0)

        @pl.when(j == 0)
        def _():
            copies = piece_copies(pieces, offs_ref, parts, w, sems)
            for copy in copies:
                copy.start()
            acc[...] = nr[...]
            for copy in copies:
                copy.wait()

        acc[...] += nt(a[...], w[:, pl.ds(pl.multiple_of(j * step, step), step)])

        @pl.when(j == n - 1)
        def _():
            out[...] = acc[...].astype(out.dtype)

    return pl.pallas_call(
        body,
        grid=(n,),
        in_specs=[
            pl.BlockSpec(memory_space=pltpu.SMEM),
            pl.BlockSpec((toks, DS), lambda j: (which, 0)),
            pl.BlockSpec((toks, step), lambda j: (which, j)),
        ]
        + [pl.BlockSpec(memory_space=pl.ANY)] * count,
        out_specs=whole((toks, DS)),
        out_shape=jax.ShapeDtypeStruct((toks, DS), dtype),
        scratch_shapes=[
            pltpu.VMEM((toks, DS), F32),
            pltpu.VMEM((DS, cols), BF16),
            pltpu.SemaphoreType.DMA((count,)),
        ],
        compiler_params=PARAMS,
        cost_estimate=TINY,
        name="branch_far",
    )(piece_offsets(pieces), near, act, *[p[0] for p in pieces])


def branch_near_part(act, weight):
    count, cols = act.shape
    step = 2 * FC

    def body(a, w, out):
        value = nt(a[...], w[...])

        @pl.when(pl.program_id(0) == 0)
        def _():
            out[...] = value

        @pl.when(pl.program_id(0) > 0)
        def _():
            out[...] += value

    return pl.pallas_call(
        body,
        grid=(cols // step,),
        in_specs=[
            pl.BlockSpec((count, step), lambda j: (0, j)),
            pl.BlockSpec((DS, step), lambda j: (0, j)),
        ],
        out_specs=whole((count, DS)),
        out_shape=jax.ShapeDtypeStruct((count, DS), F32),
        compiler_params=PARAMS,
        cost_estimate=TINY,
        name="branch_near",
    )(act, weight)


def branch_part(near, act, weight, which, dtype):
    toks = act.shape[0] // 2
    cols = act.shape[1]
    step = 2 * FC
    n = cols // step

    def body(nr, a, w, out, acc):
        j = pl.program_id(0)

        @pl.when(j == 0)
        def _():
            acc[...] = nr[...]

        acc[...] += nt(a[...], w[...])

        @pl.when(j == n - 1)
        def _():
            out[...] = acc[...].astype(out.dtype)

    return pl.pallas_call(
        body,
        grid=(n,),
        in_specs=[
            pl.BlockSpec((toks, DS), lambda j: (which, 0)),
            pl.BlockSpec((toks, step), lambda j: (which, j)),
            pl.BlockSpec((DS, step), lambda j: (0, j)),
        ],
        out_specs=whole((toks, DS)),
        out_shape=jax.ShapeDtypeStruct((toks, DS), dtype),
        scratch_shapes=[pltpu.VMEM((toks, DS), F32)],
        compiler_params=PARAMS,
        cost_estimate=TINY,
        name="branch",
    )(near, act, weight)


def store_blocks(mx, acc, scratch, outs):
    if len(outs) == 1:
        outs[0][...] = acc.astype(BF16)
        return
    rows = DS // 4
    scratch[...] = acc.astype(BF16)
    for k, out in enumerate(outs):
        off = pl.multiple_of((mx ^ k) * rows, 32)
        out[...] = scratch[pl.ds(off, rows), :]


def block_outs(split, cols):
    count, rows = (4, DS // 4) if split else (1, DS)
    specs = [pl.BlockSpec((rows, FC), lambda j: (0, j))] * count
    shapes = [jax.ShapeDtypeStruct((rows, cols), BF16)] * count
    return specs, shapes


def grad_out_part(mx, grad_own, grad_pair, act, split):
    toks = grad_own.shape[0]
    cols = act.shape[1]
    specs, shapes = block_outs(split, cols)

    def body(mx_ref, go, gp, a, *rest):
        outs, (gt, scratch) = rest[:-2], rest[-2:]

        @pl.when(pl.program_id(0) == 0)
        def _():
            gt[:, :toks] = go[...].T
            gt[:, toks:] = gp[...].T

        acc = jnp.dot(gt[...], a[...], preferred_element_type=F32)
        store_blocks(mx_ref[0], acc, scratch, outs)

    return pl.pallas_call(
        body,
        grid=(cols // FC,),
        in_specs=[
            pl.BlockSpec(memory_space=pltpu.SMEM),
            whole((toks, DS)),
            whole((toks, DS)),
            pl.BlockSpec((2 * toks, FC), lambda j: (0, j)),
        ],
        out_specs=specs,
        out_shape=shapes,
        scratch_shapes=[pltpu.VMEM((DS, 2 * toks), BF16), pltpu.VMEM((DS, FC), BF16)],
        compiler_params=LIGHT,
        cost_estimate=TINY,
        name="grad_out",
    )(mx, grad_own, grad_pair, act)


def grad_in_part(mx, grad_own, grad_pair, w_out, slope, normed_t, split):
    toks = grad_own.shape[0]
    cols = w_out.shape[1]
    specs, shapes = block_outs(split, cols)

    def body(mx_ref, go, gp, w, sl, nrm, *rest):
        outs, (pre, scratch) = rest[:-2], rest[-2:]
        for part, off in ((go, 0), (gp, toks)):
            act_grad = jnp.dot(part[...], w[...], preferred_element_type=F32)
            pre[off : off + toks, :] = (act_grad * sl[off : off + toks, :]).astype(BF16)
        acc = jnp.dot(nrm[...], pre[...], preferred_element_type=F32)
        store_blocks(mx_ref[0], acc, scratch, outs)

    return pl.pallas_call(
        body,
        grid=(cols // FC,),
        in_specs=[
            pl.BlockSpec(memory_space=pltpu.SMEM),
            whole((toks, DS)),
            whole((toks, DS)),
            pl.BlockSpec((DS, FC), lambda j: (0, j)),
            pl.BlockSpec((2 * toks, FC), lambda j: (0, j)),
            whole((DS, 2 * toks)),
        ],
        out_specs=specs,
        out_shape=shapes,
        scratch_shapes=[pltpu.VMEM((2 * toks, FC), BF16), pltpu.VMEM((DS, FC), BF16)],
        compiler_params=LIGHT,
        cost_estimate=TINY,
        name="grad_in",
    )(mx, grad_own, grad_pair, w_out, slope, normed_t)


def after(value, *deps):
    return lax.optimization_barrier((value,) + deps)[0]


def together(*values):
    return lax.optimization_barrier(values)


def nt(left, right):
    return lax.dot_general(left, right, (((1,), (1,)), ((), ())), preferred_element_type=F32)


def tn(left, right):
    return lax.dot_general(
        left, right, (((0,), (0,)), ((), ())), preferred_element_type=F32
    ).astype(BF16)


def pair_shards(teacher_feats, t_gain, t_bias, projection, student_in, s_gain, w_in, w_out):
    mx = lax.axis_index("mx")
    g = lax.axis_index("group")
    patch_all, image_loc, feat_loc = teacher_feats.shape
    patch_loc = patch_all // 4
    toks = patch_loc * image_loc
    tokens = PATCHES * image_loc * 4
    w_out = w_out.T
    rows, cols = w_in.shape
    half = rows // 2
    mine, other = g * half, (1 - g) * half

    mx1 = mx.reshape(1).astype(jnp.int32)

    def my_half(w):
        return lax.dynamic_slice(w, (mine, 0), (half, cols))

    z_send = jnp.concatenate([my_half(w_in), my_half(w_out)], axis=0)
    z_g = swap(z_send, "my", 2)
    in_near = lax.all_gather(w_in, "mx", axis=0, tiled=True)
    out_near = lax.all_gather(w_out, "mx", axis=0, tiled=True)

    feats = teacher_feats.reshape(4 * toks, feat_loc)
    student = student_in.reshape(toks, DS)
    normed_own = student_norm(after(student, z_send), s_gain.reshape(1, DS))
    normed_pair = swap(normed_own, "my", 1)
    sums = teacher_sums(after(feats, normed_own))
    sums = lax.psum(sums[:2], "mx")
    gain = t_gain.astype(F32).reshape(1, feat_loc)
    bias = t_bias.astype(F32).reshape(1, feat_loc)
    parts = target_parts(mx1, (3, 2, 1, 0), feats, sums, gain, bias, projection)
    q3, q2, q1, q0, z_g, normed_pair = together(*parts, z_g, normed_pair)

    d_g = swap(z_g, "mx", 2)
    z_o = swap(z_g, "group", 1)
    zgc = swap(z_g, "mx", 1)
    q3c = swap(q3, "mx", 1)
    pre_near, act_near = forward_part(normed_own, normed_pair, in_near)
    pre_near, act_near, d_g, z_o, zgc, q3c = together(pre_near, act_near, d_g, z_o, zgc, q3c)
    in_do = swap(d_g[:half], "group", 1)
    out_do = swap(z_o[half:], "mx", 2)
    zoc, dgc = swap(z_o, "mx", 1), swap(d_g, "mx", 1)
    t2 = (q2.astype(F32) + q3c.astype(F32)).astype(BF16)
    near_share = branch_near_part(after(act_near, t2), out_near)
    in_do, out_do, zoc, dgc, near_share = together(in_do, out_do, zoc, dgc, near_share)
    in_doc, out_doc = swap(in_do, "mx", 1), swap(out_do, "mx", 1)
    in_doc, out_doc = together(in_doc, out_doc)

    def far_rows(first, d_o, d_oc):
        out = []
        for part, part_c, block, off, at in (
            (z_g, zgc, 0, mine, first),
            (z_o, zoc, 0, other, first),
            (d_g, dgc, 2, mine, first),
            (d_o, d_oc, 2, other, 0),
        ):
            out.append((part, at, half, (mx ^ block) * rows + off))
            out.append((part_c, at, half, (mx ^ block ^ 1) * rows + off))
        return out

    target_x = swap(after(t2, in_doc), "mx", 2)
    q1c = swap(after(q1, in_doc), "mx", 1)
    pre_far, act_far = forward_pieces(normed_own, normed_pair, far_rows(0, in_do, in_doc))
    pre_far, act_far, q1c = together(pre_far, act_far, q1c)
    out_rows = far_rows(half, out_do, out_doc)
    t0 = q0.astype(F32) + q1c.astype(F32)

    branch_pair = branch_pieces(near_share, act_far, out_rows, 1, BF16)
    branch_recv = swap(branch_pair, "my", 1)
    out_far = assemble([(p, at, n, after(o, branch_pair)) for p, at, n, o in out_rows], DS)
    branch_own = branch_part(near_share, act_far, out_far, 0, F32)
    slope_far = gelu_slope(after(pre_far, branch_own))
    branch_recv = after(branch_recv, slope_far)

    target = t0 + target_x.astype(F32)
    residue = student.astype(F32) + (branch_own + branch_recv.astype(F32)) - target
    grad_own = (residue / jnp.sqrt(jnp.float32(tokens))).astype(BF16)
    loss = jnp.broadcast_to(jnp.sum(residue * residue), (8, 128))
    grad_own, loss = lax.optimization_barrier((grad_own, loss))
    grad_pair = swap(grad_own, "my", 1)
    for bit in (1, 2):
        loss = loss + swap(loss, "mx", bit)
    slope_near = gelu_slope(after(pre_near, grad_own))
    normed_t = jnp.concatenate([after(normed_own, slope_near).T, normed_pair.T], axis=1)
    grad_pair, loss, slope_near, normed_t = together(grad_pair, loss, slope_near, normed_t)

    o0, o1, o2, o3 = grad_out_part(mx1, grad_own, grad_pair, act_far, True)
    got2, got0 = swap(o3, "mx", 1), swap(o1, "mx", 1)
    early = rows // 48 * 16 + 16
    h0, h1 = slice(0, early), slice(early, rows)
    s2_out = [(o2[c].astype(F32) + got2[c].astype(F32)).astype(BF16) for c in (h0, h1)]
    x_out = [swap(v, "mx", 2) for v in s2_out]
    n0, n1, n2, n3 = grad_out_part(mx1, after(grad_own, *s2_out), grad_pair, act_near, True)
    n0, n1, n2, n3, x_out0, got0 = together(n0, n1, n2, n3, x_out[0], got0)

    def last(keep, got, x):
        return (keep.astype(F32) + got.astype(F32) + x.astype(F32)).astype(BF16)

    f0 = last(o0[h0], got0[h0], x_out0)
    f_out0 = swap(f0, "my", 2)
    gn2, gn0 = swap(after(n3, f0), "mx", 1), swap(after(n1, f0), "mx", 1)
    i0, i1, i2, i3 = grad_in_part(
        mx1, after(grad_own, f0), grad_pair, out_far, slope_far, normed_t, True
    )
    i0, i1, i2, i3, x_out1, gn2, gn0, f_out0 = together(
        i0, i1, i2, i3, x_out[1], gn2, gn0, f_out0
    )
    f1 = last(o0[h1], got0[h1], x_out1)
    f_out1 = swap(f1, "my", 2)
    gin2, gin0 = swap(i3, "mx", 1), swap(i1, "mx", 1)
    loss_z = swap(after(loss, f1), "my", 1)
    s2_on = (n2.astype(F32) + gn2.astype(F32)).astype(BF16)
    gin2, gin0, s2_on, loss_z = together(gin2, gin0, s2_on, loss_z)
    loss = loss + loss_z
    s2_in = (i2.astype(F32) + gin2.astype(F32)).astype(BF16)
    x_in = swap(s2_in, "mx", 2)
    x_on = swap(after(s2_on, s2_in), "mx", 2)
    m0, m1, m2, m3 = grad_in_part(
        mx1, after(grad_own, s2_on, s2_in), grad_pair, out_near, slope_near, normed_t, True
    )
    m0, m1, m2, m3, x_in, f_out1 = together(m0, m1, m2, m3, x_in, f_out1)
    f2 = [last(i0[c], gin0[c], x_in[c]) for c in (h0, h1)]
    f_in = [swap(v, "my", 2) for v in f2]
    gm2, gm0 = swap(after(m3, *f2), "mx", 1), swap(after(m1, *f2), "mx", 1)
    loss_z = swap(after(loss, *f2), "my", 2)
    gm2, gm0, x_on, f_in0, loss_z = together(gm2, gm0, x_on, f_in[0], loss_z)
    mse_loss = (loss + loss_z)[0, :1] / (tokens * DS)
    s2_mn = (m2.astype(F32) + gm2.astype(F32)).astype(BF16)
    x_mn = swap(s2_mn, "mx", 2)
    grad_out_near = n0.astype(F32) + gn0.astype(F32) + x_on.astype(F32)
    grad_in_near = m0.astype(F32) + gm0.astype(F32) + x_mn.astype(F32)
    f_out = jnp.concatenate([f_out0, f_out1], axis=0)
    f_in = jnp.concatenate([f_in0, f_in[1]], axis=0)
    grad_out = (grad_out_near + f_out.astype(F32)).T
    grad_in = grad_in_near + f_in.astype(F32)
    return (mse_loss, grad_in, grad_out)


def shards(teacher_feats, t_gain, t_bias, projection, student_in, s_gain, w_in, w_out):
    patch_all, image_loc, feat_loc = teacher_feats.shape
    mx_count = lax.axis_size("mx")
    my_count = lax.axis_size("my")
    patch_loc = patch_all // mx_count
    features = teacher_feats.astype(jnp.float32)
    feature_sum, squares = lax.psum(
        (jnp.sum(features, axis=2), jnp.sum(features * features, axis=2)), "mx"
    )
    row_mean = feature_sum / DT
    variance = squares / DT - row_mean * row_mean
    normed_teacher = (
        (features - row_mean[..., None])
        * lax.rsqrt(variance + epsilon)[..., None]
        * t_gain.astype(jnp.float32)
        + t_bias.astype(jnp.float32)
    ).astype(jnp.bfloat16)
    flattened = normed_teacher.reshape(patch_loc * lax.axis_size("mx") * image_loc, feat_loc)
    target = lax.psum_scatter(
        jnp.dot(flattened, projection, preferred_element_type=jnp.float32)
        .reshape(patch_loc * lax.axis_size("mx"), image_loc, DS)
        .astype(jnp.bfloat16),
        "mx",
        scatter_dimension=0,
        tiled=True,
    ).astype(jnp.float32)
    student_f32 = student_in.astype(jnp.float32)
    student_mean = jnp.sum(student_f32, axis=2, keepdims=True) / DS
    student_square = jnp.sum(student_f32 * student_f32, axis=2, keepdims=True) / DS
    normed = (
        (student_f32 - student_mean)
        * lax.rsqrt(student_square - student_mean * student_mean + epsilon)
        * s_gain
    ).astype(jnp.bfloat16)
    gathered = lax.all_gather(normed, "my", axis=1, tiled=True)
    rows_all = patch_loc * image_loc * my_count
    normed_flat = gathered.reshape(rows_all, DS)
    preact = jnp.dot(
        normed_flat,
        lax.all_gather(w_in, "mx", axis=0, tiled=True),
        preferred_element_type=jnp.float32,
    )
    activation = gelu_value(preact).astype(jnp.bfloat16)
    w_out_full = lax.all_gather(w_out, "mx", axis=1, tiled=True)
    branch_part = jnp.dot(activation, w_out_full, preferred_element_type=jnp.float32).reshape(
        patch_loc, image_loc * my_count, DS
    )
    branch = lax.psum_scatter(
        branch_part.astype(jnp.bfloat16), "my", scatter_dimension=1, tiled=True
    ).astype(jnp.float32)
    residue = student_f32 + branch - target
    tokens = PATCHES * image_loc * my_count
    squared_sum = lax.psum(jnp.sum(residue * residue), ("mx", "my"))
    mse_loss = jnp.reshape(squared_sum / (tokens * DS), (1,))
    grad_output = (residue / jnp.sqrt(jnp.float32(tokens))).astype(jnp.bfloat16)
    grad_rows = lax.all_gather(grad_output, "my", axis=1, tiled=True).reshape(rows_all, DS)
    grad_act = lax.dot_general(
        grad_rows, w_out_full, (((1,), (1,)), ((), ())), preferred_element_type=jnp.float32
    )
    grad_pre = (grad_act * gelu_slope(preact)).astype(jnp.bfloat16)
    part_in = lax.dot_general(
        normed_flat, grad_pre, (((0,), (0,)), ((), ())), preferred_element_type=jnp.float32
    )
    part_out = lax.dot_general(
        activation, grad_rows, (((0,), (0,)), ((), ())), preferred_element_type=jnp.float32
    )
    grad_in = lax.psum_scatter(
        part_in.astype(jnp.bfloat16), "mx", scatter_dimension=0, tiled=True
    ).astype(jnp.float32)
    grad_out = lax.psum_scatter(
        part_out.astype(jnp.bfloat16), "mx", scatter_dimension=1, tiled=True
    ).astype(jnp.float32)
    return (mse_loss, grad_in, grad_out)


def solution(mesh):
    in_specs = (
        P(None, ("group", "my"), "mx"),
        P("mx"),
        P("mx"),
        P("mx", None),
        P("mx", ("group", "my"), None),
        P(),
        P("mx", "my"),
        P("my", "mx"),
    )
    out_specs = (P("group"), P(("group", "mx"), "my"), P(("group", "my"), "mx"))
    pairs = mesh.shape["group"] == 2 and mesh.shape["mx"] == 4 and mesh.shape["my"] == 4
    body = pair_shards if pairs else shards
    return jax.shard_map(body, mesh=mesh, in_specs=in_specs, out_specs=out_specs, check_vma=False)
```

```python
import jax
import jax.numpy as jnp
from jax import lax
from jax.experimental import pallas as pl
from jax.experimental.pallas import tpu as pltpu
from jax.sharding import PartitionSpec as P

DT = 6144
DS = 1408
PATCHES = 256
F32 = jnp.float32
BF16 = jnp.bfloat16

epsilon = 1e-06

FC = 256
TINY = pl.CostEstimate(flops=1000, transcendentals=0, bytes_accessed=1000)
PARAMS = pltpu.CompilerParams(vmem_limit_bytes=58 * 2**20)
LIGHT = pltpu.CompilerParams(vmem_limit_bytes=24 * 2**20)


def gelu_value(value):
    return 0.5 * value * (1.0 + lax.erf(value * 0.7071067811865476))


def gelu_slope(value):
    return (
        0.5 * (1.0 + lax.erf(value * 0.7071067811865476))
        + value * jnp.exp(-0.5 * value * value) * 0.3989422804014327
    )


def swap(value, axis, bit):
    count = lax.axis_size(axis)
    return lax.ppermute(value, axis, [(i, i ^ bit) for i in range(count)])


def piece_copies(pieces, offs_ref, parts, out, sems):
    copies = []
    for i, part in enumerate(parts):
        first, count = pieces[i][1:3]
        off = pl.multiple_of(offs_ref[i], 16)
        copies.append(
            pltpu.make_async_copy(
                part.at[first : first + count, :], out.at[pl.ds(off, count), :], sems.at[i]
            )
        )
    return copies


def piece_offsets(pieces):
    return jnp.stack([jnp.asarray(p[3], jnp.int32) for p in pieces])


def assemble(pieces, rows):
    arrays = [p[0] for p in pieces]
    cols = arrays[0].shape[1]
    offs = piece_offsets(pieces)

    def body(offs_ref, *refs):
        parts, out, sems = refs[:-2], refs[-2], refs[-1]
        copies = piece_copies(pieces, offs_ref, parts, out, sems)
        for copy in copies:
            copy.start()
        for copy in copies:
            copy.wait()

    return pl.pallas_call(
        body,
        out_shape=jax.ShapeDtypeStruct((rows, cols), arrays[0].dtype),
        in_specs=[pl.BlockSpec(memory_space=pltpu.SMEM)]
        + [pl.BlockSpec(memory_space=pl.ANY)] * len(pieces),
        out_specs=pl.BlockSpec(memory_space=pltpu.VMEM),
        scratch_shapes=[pltpu.SemaphoreType.DMA((len(pieces),))],
        cost_estimate=TINY,
        compiler_params=PARAMS,
        name="assemble",
    )(offs, *arrays)


def whole(shape):
    return pl.BlockSpec(shape, lambda j: (0,) * len(shape))


def turned(value):
    part = value[:, :128]
    for at in range(128, value.shape[1], 128):
        part = part + value[:, at : at + 128]
    return jnp.sum(part.T, axis=0, keepdims=True)


def teacher_sums(feats):
    count, width = feats.shape
    step = 512

    def body(x_ref, out):
        x = x_ref[...].astype(F32)
        out[0:1, :] = turned(x)
        out[1:2, :] = turned(x * x)
        out[2:, :] = jnp.zeros((6, step), F32)

    return pl.pallas_call(
        body,
        grid=(count // step,),
        in_specs=[pl.BlockSpec((step, width), lambda j: (j, 0))],
        out_specs=pl.BlockSpec((8, step), lambda j: (0, j)),
        out_shape=jax.ShapeDtypeStruct((8, count), F32),
        compiler_params=PARAMS,
        cost_estimate=TINY,
        name="teacher_sums",
    )(feats)


def target_parts(mx, ks, feats, sums, gain, bias, projection):
    count, width = feats.shape
    step = 256
    toks = count // 4
    per = toks // step

    def body(mx_ref, x_ref, s_ref, g_ref, b_ref, w_ref, *outs):
        j = pl.program_id(0)
        sums_t = jnp.concatenate([s_ref[...], jnp.zeros((6, step), F32)], axis=0).T
        mean = sums_t[:, 0:1] / DT
        rstd = lax.rsqrt(sums_t[:, 1:2] / DT - mean * mean + epsilon)
        tnorm = (x_ref[...].astype(F32) - mean) * rstd * g_ref[...] + b_ref[...]
        value = jnp.dot(tnorm.astype(BF16), w_ref[...], preferred_element_type=F32).astype(BF16)
        for n, out in enumerate(outs):

            @pl.when(j // per == n)
            def _(out=out):
                out[...] = value

    def row(j, mx_ref):
        k = ks[0] - j // per
        return (mx_ref[0] ^ k) * per + j % per

    return pl.pallas_call(
        body,
        grid_spec=pltpu.PrefetchScalarGridSpec(
            num_scalar_prefetch=1,
            grid=(len(ks) * per,),
            in_specs=[
                pl.BlockSpec((step, width), lambda j, m: (row(j, m), 0)),
                pl.BlockSpec((2, step), lambda j, m: (0, row(j, m))),
                pl.BlockSpec((1, width), lambda j, m: (0, 0)),
                pl.BlockSpec((1, width), lambda j, m: (0, 0)),
                pl.BlockSpec((width, DS), lambda j, m: (0, 0)),
            ],
            out_specs=[
                pl.BlockSpec(
                    (step, DS), lambda j, m, n=n: (jnp.clip(j - n * per, 0, per - 1), 0)
                )
                for n in range(len(ks))
            ],
        ),
        out_shape=[jax.ShapeDtypeStruct((toks, DS), BF16)] * len(ks),
        compiler_params=PARAMS,
        cost_estimate=TINY,
        name="targets",
    )(mx, feats, sums, gain, bias, projection)


def student_norm(student, gain):
    count, width = student.shape
    step = 128

    def body(x_ref, g_ref, out):
        x = x_ref[...].astype(F32)
        mean = jnp.sum(x, axis=1, keepdims=True) / DS
        square = jnp.sum(x * x, axis=1, keepdims=True) / DS
        out[...] = ((x - mean) * lax.rsqrt(square - mean * mean + epsilon) * g_ref[...]).astype(BF16)

    return pl.pallas_call(
        body,
        grid=(count // step,),
        in_specs=[
            pl.BlockSpec((step, width), lambda j: (j, 0)),
            pl.BlockSpec((1, width), lambda j: (0, 0)),
        ],
        out_specs=pl.BlockSpec((step, width), lambda j: (j, 0)),
        out_shape=jax.ShapeDtypeStruct((count, width), BF16),
        compiler_params=LIGHT,
        cost_estimate=TINY,
        name="student_norm",
    )(student, gain)


def forward_part(normed_own, normed_pair, weight):
    toks = normed_own.shape[0]
    cols = weight.shape[-1]

    def body(no, np_, w, pre, act):
        for part, off in ((no, 0), (np_, toks)):
            value = jnp.dot(part[...], flat(w), preferred_element_type=F32)
            pre[off : off + toks, :] = value
            act[off : off + toks, :] = gelu_value(value).astype(BF16)

    chunk = pl.BlockSpec((2 * toks, FC), lambda j: (0, j))
    return pl.pallas_call(
        body,
        grid=(cols // FC,),
        in_specs=[whole((toks, DS)), whole((toks, DS)), weight_spec(weight, 0, FC)],
        out_specs=[chunk, chunk],
        out_shape=[
            jax.ShapeDtypeStruct((2 * toks, cols), F32),
            jax.ShapeDtypeStruct((2 * toks, cols), BF16),
        ],
        compiler_params=PARAMS,
        cost_estimate=TINY,
        name="forward",
    )(normed_own, normed_pair, weight)


def forward_pieces(normed_own, normed_pair, pieces):
    toks = normed_own.shape[0]
    cols = pieces[0][0].shape[1]
    count = len(pieces)

    def body(offs_ref, no, np_, *refs):
        parts, (pre, act, w, sems) = refs[:count], refs[count:]
        j = pl.program_id(0)

        @pl.when(j == 0)
        def _():
            copies = piece_copies(pieces, offs_ref, parts, w, sems)
            for copy in copies:
                copy.start()
            for copy in copies:
                copy.wait()

        chunk = w[:, pl.ds(pl.multiple_of(j * FC, FC), FC)]
        for part, off in ((no, 0), (np_, toks)):
            value = jnp.dot(part[...], chunk, preferred_element_type=F32)
            pre[off : off + toks, :] = value
            act[off : off + toks, :] = gelu_value(value).astype(BF16)

    chunk = pl.BlockSpec((2 * toks, FC), lambda j: (0, j))
    return pl.pallas_call(
        body,
        grid=(cols // FC,),
        in_specs=[pl.BlockSpec(memory_space=pltpu.SMEM), whole((toks, DS)), whole((toks, DS))]
        + [pl.BlockSpec(memory_space=pl.ANY)] * count,
        out_specs=[chunk, chunk],
        out_shape=[
            jax.ShapeDtypeStruct((2 * toks, cols), F32),
            jax.ShapeDtypeStruct((2 * toks, cols), BF16),
        ],
        scratch_shapes=[pltpu.VMEM((DS, cols), BF16), pltpu.SemaphoreType.DMA((count,))],
        compiler_params=PARAMS,
        cost_estimate=TINY,
        name="forward_far",
    )(piece_offsets(pieces), normed_own, normed_pair, *[p[0] for p in pieces])


def branch_pieces(near, act, pieces, which, dtype):
    toks = act.shape[0] // 2
    cols = act.shape[1]
    step = 2 * FC
    n = cols // step
    count = len(pieces)

    def body(offs_ref, nr, a, *refs):
        parts, (out, acc, w, sems) = refs[:count], refs[count:]
        j = pl.program_id(0)

        @pl.when(j == 0)
        def _():
            copies = piece_copies(pieces, offs_ref, parts, w, sems)
            for copy in copies:
                copy.start()
            acc[...] = nr[...]
            for copy in copies:
                copy.wait()

        acc[...] += nt(a[...], w[:, pl.ds(pl.multiple_of(j * step, step), step)])

        @pl.when(j == n - 1)
        def _():
            out[...] = acc[...].astype(out.dtype)

    return pl.pallas_call(
        body,
        grid=(n,),
        in_specs=[
            pl.BlockSpec(memory_space=pltpu.SMEM),
            pl.BlockSpec((toks, DS), lambda j: (which, 0)),
            pl.BlockSpec((toks, step), lambda j: (which, j)),
        ]
        + [pl.BlockSpec(memory_space=pl.ANY)] * count,
        out_specs=whole((toks, DS)),
        out_shape=jax.ShapeDtypeStruct((toks, DS), dtype),
        scratch_shapes=[
            pltpu.VMEM((toks, DS), F32),
            pltpu.VMEM((DS, cols), BF16),
            pltpu.SemaphoreType.DMA((count,)),
        ],
        compiler_params=PARAMS,
        cost_estimate=TINY,
        name="branch_far",
    )(piece_offsets(pieces), near, act, *[p[0] for p in pieces])


def weight_spec(weight, which, width):
    if weight.ndim == 2:
        return pl.BlockSpec((DS, width), lambda j: (0, j))
    return pl.BlockSpec((4, 1, DS // 4, width), lambda j: (0, which, 0, j))


def flat(w):
    return w[...].reshape(DS, w.shape[-1])


def branch_near_part(act, weight):
    count, cols = act.shape
    step = 2 * FC

    def body(a, w, out):
        value = nt(a[...], flat(w))

        @pl.when(pl.program_id(0) == 0)
        def _():
            out[...] = value

        @pl.when(pl.program_id(0) > 0)
        def _():
            out[...] += value

    return pl.pallas_call(
        body,
        grid=(cols // step,),
        in_specs=[
            pl.BlockSpec((count, step), lambda j: (0, j)),
            weight_spec(weight, 1, step),
        ],
        out_specs=whole((count, DS)),
        out_shape=jax.ShapeDtypeStruct((count, DS), F32),
        compiler_params=PARAMS,
        cost_estimate=TINY,
        name="branch_near",
    )(act, weight)


def branch_part(near, act, weight, which, dtype):
    toks = act.shape[0] // 2
    cols = act.shape[1]
    step = 2 * FC
    n = cols // step

    def body(nr, a, w, out, acc):
        j = pl.program_id(0)

        @pl.when(j == 0)
        def _():
            acc[...] = nr[...]

        acc[...] += nt(a[...], w[...])

        @pl.when(j == n - 1)
        def _():
            out[...] = acc[...].astype(out.dtype)

    return pl.pallas_call(
        body,
        grid=(n,),
        in_specs=[
            pl.BlockSpec((toks, DS), lambda j: (which, 0)),
            pl.BlockSpec((toks, step), lambda j: (which, j)),
            pl.BlockSpec((DS, step), lambda j: (0, j)),
        ],
        out_specs=whole((toks, DS)),
        out_shape=jax.ShapeDtypeStruct((toks, DS), dtype),
        scratch_shapes=[pltpu.VMEM((toks, DS), F32)],
        compiler_params=PARAMS,
        cost_estimate=TINY,
        name="branch",
    )(near, act, weight)


def store_blocks(mx, acc, scratch, outs):
    if len(outs) == 1:
        outs[0][...] = acc.astype(BF16)
        return
    rows = DS // 4
    scratch[...] = acc.astype(BF16)
    for k, out in enumerate(outs):
        off = pl.multiple_of((mx ^ k) * rows, 32)
        out[...] = scratch[pl.ds(off, rows), :]


def block_outs(split, cols):
    count, rows = (4, DS // 4) if split else (1, DS)
    specs = [pl.BlockSpec((rows, FC), lambda j: (0, j))] * count
    shapes = [jax.ShapeDtypeStruct((rows, cols), BF16)] * count
    return specs, shapes


def grad_out_part(mx, grad_own, grad_pair, act, split):
    toks = grad_own.shape[0]
    cols = act.shape[1]
    specs, shapes = block_outs(split, cols)

    def body(mx_ref, go, gp, a, *rest):
        outs, (gt, scratch) = rest[:-2], rest[-2:]

        @pl.when(pl.program_id(0) == 0)
        def _():
            gt[:, :toks] = go[...].T
            gt[:, toks:] = gp[...].T

        acc = jnp.dot(gt[...], a[...], preferred_element_type=F32)
        store_blocks(mx_ref[0], acc, scratch, outs)

    return pl.pallas_call(
        body,
        grid=(cols // FC,),
        in_specs=[
            pl.BlockSpec(memory_space=pltpu.SMEM),
            whole((toks, DS)),
            whole((toks, DS)),
            pl.BlockSpec((2 * toks, FC), lambda j: (0, j)),
        ],
        out_specs=specs,
        out_shape=shapes,
        scratch_shapes=[pltpu.VMEM((DS, 2 * toks), BF16), pltpu.VMEM((DS, FC), BF16)],
        compiler_params=LIGHT,
        cost_estimate=TINY,
        name="grad_out",
    )(mx, grad_own, grad_pair, act)


def grad_in_part(mx, grad_own, grad_pair, w_out, slope, normed_t, split):
    toks = grad_own.shape[0]
    cols = w_out.shape[-1]
    specs, shapes = block_outs(split, cols)

    def body(mx_ref, go, gp, w, sl, nrm, *rest):
        outs, (pre, scratch) = rest[:-2], rest[-2:]
        for part, off in ((go, 0), (gp, toks)):
            act_grad = jnp.dot(part[...], flat(w), preferred_element_type=F32)
            pre[off : off + toks, :] = (act_grad * sl[off : off + toks, :]).astype(BF16)
        acc = jnp.dot(nrm[...], pre[...], preferred_element_type=F32)
        store_blocks(mx_ref[0], acc, scratch, outs)

    return pl.pallas_call(
        body,
        grid=(cols // FC,),
        in_specs=[
            pl.BlockSpec(memory_space=pltpu.SMEM),
            whole((toks, DS)),
            whole((toks, DS)),
            weight_spec(w_out, 1, FC),
            pl.BlockSpec((2 * toks, FC), lambda j: (0, j)),
            whole((DS, 2 * toks)),
        ],
        out_specs=specs,
        out_shape=shapes,
        scratch_shapes=[pltpu.VMEM((2 * toks, FC), BF16), pltpu.VMEM((DS, FC), BF16)],
        compiler_params=LIGHT,
        cost_estimate=TINY,
        name="grad_in",
    )(mx, grad_own, grad_pair, w_out, slope, normed_t)


def after(value, *deps):
    return lax.optimization_barrier((value,) + deps)[0]


def together(*values):
    return lax.optimization_barrier(values)


def nt(left, right):
    return lax.dot_general(left, right, (((1,), (1,)), ((), ())), preferred_element_type=F32)


def tn(left, right):
    return lax.dot_general(
        left, right, (((0,), (0,)), ((), ())), preferred_element_type=F32
    ).astype(BF16)


def pair_shards(teacher_feats, t_gain, t_bias, projection, student_in, s_gain, w_in, w_out):
    mx = lax.axis_index("mx")
    g = lax.axis_index("group")
    patch_all, image_loc, feat_loc = teacher_feats.shape
    patch_loc = patch_all // 4
    toks = patch_loc * image_loc
    tokens = PATCHES * image_loc * 4
    w_out = w_out.T
    rows, cols = w_in.shape
    half = rows // 2
    mine, other = g * half, (1 - g) * half

    mx1 = mx.reshape(1).astype(jnp.int32)

    def my_half(w):
        return lax.dynamic_slice(w, (mine, 0), (half, cols))

    z_send = jnp.concatenate([my_half(w_in), my_half(w_out)], axis=0)
    z_g = swap(z_send, "my", 2)
    near = lax.all_gather(jnp.concatenate([w_in, w_out], axis=0), "mx", axis=0, tiled=True)
    near = near.reshape(4, 2, rows, cols)

    feats = teacher_feats.reshape(4 * toks, feat_loc)
    student = student_in.reshape(toks, DS)
    normed_own = student_norm(after(student, z_send), s_gain.reshape(1, DS))
    normed_pair = swap(normed_own, "my", 1)
    sums = teacher_sums(after(feats, normed_own))
    sums = lax.psum(sums[:2], "mx")
    gain = t_gain.astype(F32).reshape(1, feat_loc)
    bias = t_bias.astype(F32).reshape(1, feat_loc)
    parts = target_parts(mx1, (3, 2, 1, 0), feats, sums, gain, bias, projection)
    q3, q2, q1, q0, z_g, normed_pair = together(*parts, z_g, normed_pair)

    d_g = swap(z_g, "mx", 2)
    z_o = swap(z_g, "group", 1)
    zgc = swap(z_g, "mx", 1)
    q3c = swap(q3, "mx", 1)
    pre_near, act_near = forward_part(normed_own, normed_pair, near)
    pre_near, act_near, d_g, z_o, zgc, q3c = together(pre_near, act_near, d_g, z_o, zgc, q3c)
    in_do = swap(d_g[:half], "group", 1)
    out_do = swap(z_o[half:], "mx", 2)
    zoc, dgc = swap(z_o, "mx", 1), swap(d_g, "mx", 1)
    t2 = (q2.astype(F32) + q3c.astype(F32)).astype(BF16)
    near_share = branch_near_part(after(act_near, t2), near)
    in_do, out_do, zoc, dgc, near_share = together(in_do, out_do, zoc, dgc, near_share)
    in_doc, out_doc = swap(in_do, "mx", 1), swap(out_do, "mx", 1)
    in_doc, out_doc = together(in_doc, out_doc)

    def far_rows(first, d_o, d_oc):
        out = []
        for part, part_c, block, off, at in (
            (z_g, zgc, 0, mine, first),
            (z_o, zoc, 0, other, first),
            (d_g, dgc, 2, mine, first),
            (d_o, d_oc, 2, other, 0),
        ):
            out.append((part, at, half, (mx ^ block) * rows + off))
            out.append((part_c, at, half, (mx ^ block ^ 1) * rows + off))
        return out

    target_x = swap(after(t2, in_doc), "mx", 2)
    q1c = swap(after(q1, in_doc), "mx", 1)
    pre_far, act_far = forward_pieces(normed_own, normed_pair, far_rows(0, in_do, in_doc))
    pre_far, act_far, q1c = together(pre_far, act_far, q1c)
    out_rows = far_rows(half, out_do, out_doc)
    t0 = q0.astype(F32) + q1c.astype(F32)

    branch_pair = branch_pieces(near_share, act_far, out_rows, 1, BF16)
    branch_recv = swap(branch_pair, "my", 1)
    out_far = assemble([(p, at, n, after(o, branch_pair)) for p, at, n, o in out_rows], DS)
    branch_own = branch_part(near_share, act_far, out_far, 0, F32)
    slope_far = gelu_slope(after(pre_far, branch_own))
    branch_recv = after(branch_recv, slope_far)

    target = t0 + target_x.astype(F32)
    residue = student.astype(F32) + (branch_own + branch_recv.astype(F32)) - target
    grad_own = (residue / jnp.sqrt(jnp.float32(tokens))).astype(BF16)
    loss = jnp.broadcast_to(jnp.sum(residue * residue), (8, 128))
    grad_own, loss = lax.optimization_barrier((grad_own, loss))
    grad_pair = swap(grad_own, "my", 1)
    for bit in (1, 2):
        loss = loss + swap(loss, "mx", bit)
    slope_near = gelu_slope(after(pre_near, grad_own))
    normed_t = jnp.concatenate([after(normed_own, slope_near).T, normed_pair.T], axis=1)
    grad_pair, loss, slope_near, normed_t = together(grad_pair, loss, slope_near, normed_t)

    o0, o1, o2, o3 = grad_out_part(mx1, grad_own, grad_pair, act_far, True)
    got2, got0 = swap(o3, "mx", 1), swap(o1, "mx", 1)
    early = rows // 48 * 16 + 16
    h0, h1 = slice(0, early), slice(early, rows)
    s2_out = [(o2[c].astype(F32) + got2[c].astype(F32)).astype(BF16) for c in (h0, h1)]
    x_out = [swap(v, "mx", 2) for v in s2_out]
    n0, n1, n2, n3 = grad_out_part(mx1, after(grad_own, *s2_out), grad_pair, act_near, True)
    n0, n1, n2, n3, x_out0, got0 = together(n0, n1, n2, n3, x_out[0], got0)

    def last(keep, got, x):
        return (keep.astype(F32) + got.astype(F32) + x.astype(F32)).astype(BF16)

    f0 = last(o0[h0], got0[h0], x_out0)
    f_out0 = swap(f0, "my", 2)
    gn2, gn0 = swap(after(n3, f0), "mx", 1), swap(after(n1, f0), "mx", 1)
    i0, i1, i2, i3 = grad_in_part(
        mx1, after(grad_own, f0), grad_pair, out_far, slope_far, normed_t, True
    )
    i0, i1, i2, i3, x_out1, gn2, gn0, f_out0 = together(
        i0, i1, i2, i3, x_out[1], gn2, gn0, f_out0
    )
    f1 = last(o0[h1], got0[h1], x_out1)
    f_out1, f_out2 = (swap(f1[c], "my", 2) for c in (slice(0, 48), slice(48, None)))
    gin2, gin0 = swap(i3, "mx", 1), swap(i1, "mx", 1)
    loss_z = swap(after(loss, f1), "my", 1)
    s2_on = (n2.astype(F32) + gn2.astype(F32)).astype(BF16)
    gin2, gin0, s2_on, loss_z, f_out1 = together(gin2, gin0, s2_on, loss_z, f_out1)
    loss = loss + loss_z
    s2_in = (i2.astype(F32) + gin2.astype(F32)).astype(BF16)
    x_in = swap(s2_in, "mx", 2)
    x_on = swap(after(s2_on, s2_in), "mx", 2)
    m0, m1, m2, m3 = grad_in_part(
        mx1, after(grad_own, s2_on, s2_in), grad_pair, near, slope_near, normed_t, True
    )
    m0, m1, m2, m3, x_in, f_out2 = together(m0, m1, m2, m3, x_in, f_out2)
    f2 = [last(i0[c], gin0[c], x_in[c]) for c in (h0, h1)]
    f_in = [swap(v, "my", 2) for v in f2]
    gm2, gm0 = swap(after(m3, *f2), "mx", 1), swap(after(m1, *f2), "mx", 1)
    loss_z = swap(after(loss, *f2), "my", 2)
    gm2, gm0, x_on, f_in0, loss_z = together(gm2, gm0, x_on, f_in[0], loss_z)
    mse_loss = (loss + loss_z)[0, :1] / (tokens * DS)
    s2_mn = (m2.astype(F32) + gm2.astype(F32)).astype(BF16)
    x_mn = swap(s2_mn, "mx", 2)
    grad_out_near = n0.astype(F32) + gn0.astype(F32) + x_on.astype(F32)
    grad_in_near = m0.astype(F32) + gm0.astype(F32) + x_mn.astype(F32)
    f_out = jnp.concatenate([f_out0, f_out1, f_out2], axis=0)
    f_in = jnp.concatenate([f_in0, f_in[1]], axis=0)
    grad_out = (grad_out_near + f_out.astype(F32)).T
    grad_in = grad_in_near + f_in.astype(F32)
    return (mse_loss, grad_in, grad_out)


def shards(teacher_feats, t_gain, t_bias, projection, student_in, s_gain, w_in, w_out):
    patch_all, image_loc, feat_loc = teacher_feats.shape
    mx_count = lax.axis_size("mx")
    my_count = lax.axis_size("my")
    patch_loc = patch_all // mx_count
    features = teacher_feats.astype(jnp.float32)
    feature_sum, squares = lax.psum(
        (jnp.sum(features, axis=2), jnp.sum(features * features, axis=2)), "mx"
    )
    row_mean = feature_sum / DT
    variance = squares / DT - row_mean * row_mean
    normed_teacher = (
        (features - row_mean[..., None])
        * lax.rsqrt(variance + epsilon)[..., None]
        * t_gain.astype(jnp.float32)
        + t_bias.astype(jnp.float32)
    ).astype(jnp.bfloat16)
    flattened = normed_teacher.reshape(patch_loc * lax.axis_size("mx") * image_loc, feat_loc)
    target = lax.psum_scatter(
        jnp.dot(flattened, projection, preferred_element_type=jnp.float32)
        .reshape(patch_loc * lax.axis_size("mx"), image_loc, DS)
        .astype(jnp.bfloat16),
        "mx",
        scatter_dimension=0,
        tiled=True,
    ).astype(jnp.float32)
    student_f32 = student_in.astype(jnp.float32)
    student_mean = jnp.sum(student_f32, axis=2, keepdims=True) / DS
    student_square = jnp.sum(student_f32 * student_f32, axis=2, keepdims=True) / DS
    normed = (
        (student_f32 - student_mean)
        * lax.rsqrt(student_square - student_mean * student_mean + epsilon)
        * s_gain
    ).astype(jnp.bfloat16)
    gathered = lax.all_gather(normed, "my", axis=1, tiled=True)
    rows_all = patch_loc * image_loc * my_count
    normed_flat = gathered.reshape(rows_all, DS)
    preact = jnp.dot(
        normed_flat,
        lax.all_gather(w_in, "mx", axis=0, tiled=True),
        preferred_element_type=jnp.float32,
    )
    activation = gelu_value(preact).astype(jnp.bfloat16)
    w_out_full = lax.all_gather(w_out, "mx", axis=1, tiled=True)
    branch_part = jnp.dot(activation, w_out_full, preferred_element_type=jnp.float32).reshape(
        patch_loc, image_loc * my_count, DS
    )
    branch = lax.psum_scatter(
        branch_part.astype(jnp.bfloat16), "my", scatter_dimension=1, tiled=True
    ).astype(jnp.float32)
    residue = student_f32 + branch - target
    tokens = PATCHES * image_loc * my_count
    squared_sum = lax.psum(jnp.sum(residue * residue), ("mx", "my"))
    mse_loss = jnp.reshape(squared_sum / (tokens * DS), (1,))
    grad_output = (residue / jnp.sqrt(jnp.float32(tokens))).astype(jnp.bfloat16)
    grad_rows = lax.all_gather(grad_output, "my", axis=1, tiled=True).reshape(rows_all, DS)
    grad_act = lax.dot_general(
        grad_rows, w_out_full, (((1,), (1,)), ((), ())), preferred_element_type=jnp.float32
    )
    grad_pre = (grad_act * gelu_slope(preact)).astype(jnp.bfloat16)
    part_in = lax.dot_general(
        normed_flat, grad_pre, (((0,), (0,)), ((), ())), preferred_element_type=jnp.float32
    )
    part_out = lax.dot_general(
        activation, grad_rows, (((0,), (0,)), ((), ())), preferred_element_type=jnp.float32
    )
    grad_in = lax.psum_scatter(
        part_in.astype(jnp.bfloat16), "mx", scatter_dimension=0, tiled=True
    ).astype(jnp.float32)
    grad_out = lax.psum_scatter(
        part_out.astype(jnp.bfloat16), "mx", scatter_dimension=1, tiled=True
    ).astype(jnp.float32)
    return (mse_loss, grad_in, grad_out)


def solution(mesh):
    in_specs = (
        P(None, ("group", "my"), "mx"),
        P("mx"),
        P("mx"),
        P("mx", None),
        P("mx", ("group", "my"), None),
        P(),
        P("mx", "my"),
        P("my", "mx"),
    )
    out_specs = (P("group"), P(("group", "mx"), "my"), P(("group", "my"), "mx"))
    pairs = mesh.shape["group"] == 2 and mesh.shape["mx"] == 4 and mesh.shape["my"] == 4
    body = pair_shards if pairs else shards
    return jax.shard_map(body, mesh=mesh, in_specs=in_specs, out_specs=out_specs, check_vma=False)
```

```python
import jax
import jax.numpy as jnp
from jax import lax
from jax.experimental import pallas as pl
from jax.experimental.pallas import tpu as pltpu
from jax.sharding import PartitionSpec as P

DT = 6144
DS = 1408
PATCHES = 256
F32 = jnp.float32
BF16 = jnp.bfloat16

epsilon = 1e-06

FC = 256
TINY = pl.CostEstimate(flops=1000, transcendentals=0, bytes_accessed=1000)
PARAMS = pltpu.CompilerParams(vmem_limit_bytes=58 * 2**20)
LIGHT = pltpu.CompilerParams(vmem_limit_bytes=24 * 2**20)


def gelu_value(value):
    return 0.5 * value * (1.0 + lax.erf(value * 0.7071067811865476))


def gelu_slope(value):
    return (
        0.5 * (1.0 + lax.erf(value * 0.7071067811865476))
        + value * jnp.exp(-0.5 * value * value) * 0.3989422804014327
    )


def swap(value, axis, bit):
    count = lax.axis_size(axis)
    return lax.ppermute(value, axis, [(i, i ^ bit) for i in range(count)])


def piece_copies(pieces, offs_ref, parts, out, sems):
    copies = []
    for i, part in enumerate(parts):
        first, count = pieces[i][1:3]
        off = pl.multiple_of(offs_ref[i], 16)
        copies.append(
            pltpu.make_async_copy(
                part.at[first : first + count, :], out.at[pl.ds(off, count), :], sems.at[i]
            )
        )
    return copies


def piece_offsets(pieces):
    return jnp.stack([jnp.asarray(p[3], jnp.int32) for p in pieces])


def assemble(pieces, rows):
    arrays = [p[0] for p in pieces]
    cols = arrays[0].shape[1]
    offs = piece_offsets(pieces)

    def body(offs_ref, *refs):
        parts, out, sems = refs[:-2], refs[-2], refs[-1]
        copies = piece_copies(pieces, offs_ref, parts, out, sems)
        for copy in copies:
            copy.start()
        for copy in copies:
            copy.wait()

    return pl.pallas_call(
        body,
        out_shape=jax.ShapeDtypeStruct((rows, cols), arrays[0].dtype),
        in_specs=[pl.BlockSpec(memory_space=pltpu.SMEM)]
        + [pl.BlockSpec(memory_space=pl.ANY)] * len(pieces),
        out_specs=pl.BlockSpec(memory_space=pltpu.VMEM),
        scratch_shapes=[pltpu.SemaphoreType.DMA((len(pieces),))],
        cost_estimate=TINY,
        compiler_params=PARAMS,
        name="assemble",
    )(offs, *arrays)


def whole(shape):
    return pl.BlockSpec(shape, lambda j: (0,) * len(shape))


def turned(value):
    part = value[:, :128]
    for at in range(128, value.shape[1], 128):
        part = part + value[:, at : at + 128]
    return jnp.sum(part.T, axis=0, keepdims=True)


def teacher_sums(feats):
    count, width = feats.shape
    step = 512

    def body(x_ref, out):
        x = x_ref[...].astype(F32)
        out[0:1, :] = turned(x)
        out[1:2, :] = turned(x * x)
        out[2:, :] = jnp.zeros((6, step), F32)

    return pl.pallas_call(
        body,
        grid=(count // step,),
        in_specs=[pl.BlockSpec((step, width), lambda j: (j, 0))],
        out_specs=pl.BlockSpec((8, step), lambda j: (0, j)),
        out_shape=jax.ShapeDtypeStruct((8, count), F32),
        compiler_params=PARAMS,
        cost_estimate=TINY,
        name="teacher_sums",
    )(feats)


def target_parts(mx, ks, feats, sums, gain, bias, projection):
    count, width = feats.shape
    step = 256
    toks = count // 4
    per = toks // step

    def body(mx_ref, x_ref, s_ref, g_ref, b_ref, w_ref, *outs):
        j = pl.program_id(0)
        sums_t = jnp.concatenate([s_ref[...], jnp.zeros((6, step), F32)], axis=0).T
        mean = sums_t[:, 0:1] / DT
        rstd = lax.rsqrt(sums_t[:, 1:2] / DT - mean * mean + epsilon)
        tnorm = (x_ref[...].astype(F32) - mean) * rstd * g_ref[...] + b_ref[...]
        value = jnp.dot(tnorm.astype(BF16), w_ref[...], preferred_element_type=F32).astype(BF16)
        for n, out in enumerate(outs):

            @pl.when(j // per == n)
            def _(out=out):
                out[...] = value

    def row(j, mx_ref):
        k = ks[0] - j // per
        return (mx_ref[0] ^ k) * per + j % per

    return pl.pallas_call(
        body,
        grid_spec=pltpu.PrefetchScalarGridSpec(
            num_scalar_prefetch=1,
            grid=(len(ks) * per,),
            in_specs=[
                pl.BlockSpec((step, width), lambda j, m: (row(j, m), 0)),
                pl.BlockSpec((2, step), lambda j, m: (0, row(j, m))),
                pl.BlockSpec((1, width), lambda j, m: (0, 0)),
                pl.BlockSpec((1, width), lambda j, m: (0, 0)),
                pl.BlockSpec((width, DS), lambda j, m: (0, 0)),
            ],
            out_specs=[
                pl.BlockSpec(
                    (step, DS), lambda j, m, n=n: (jnp.clip(j - n * per, 0, per - 1), 0)
                )
                for n in range(len(ks))
            ],
        ),
        out_shape=[jax.ShapeDtypeStruct((toks, DS), BF16)] * len(ks),
        compiler_params=PARAMS,
        cost_estimate=TINY,
        name="targets",
    )(mx, feats, sums, gain, bias, projection)


def student_norm(student, gain):
    count, width = student.shape
    step = 128

    def body(x_ref, g_ref, out):
        x = x_ref[...].astype(F32)
        mean = jnp.sum(x, axis=1, keepdims=True) / DS
        square = jnp.sum(x * x, axis=1, keepdims=True) / DS
        out[...] = ((x - mean) * lax.rsqrt(square - mean * mean + epsilon) * g_ref[...]).astype(BF16)

    return pl.pallas_call(
        body,
        grid=(count // step,),
        in_specs=[
            pl.BlockSpec((step, width), lambda j: (j, 0)),
            pl.BlockSpec((1, width), lambda j: (0, 0)),
        ],
        out_specs=pl.BlockSpec((step, width), lambda j: (j, 0)),
        out_shape=jax.ShapeDtypeStruct((count, width), BF16),
        compiler_params=LIGHT,
        cost_estimate=TINY,
        name="student_norm",
    )(student, gain)


def forward_part(normed_own, normed_pair, weight):
    toks = normed_own.shape[0]
    cols = weight.shape[-1]

    def body(no, np_, w, pre, act):
        for part, off in ((no, 0), (np_, toks)):
            value = jnp.dot(part[...], flat(w), preferred_element_type=F32)
            pre[off : off + toks, :] = value
            act[off : off + toks, :] = gelu_value(value).astype(BF16)

    chunk = pl.BlockSpec((2 * toks, FC), lambda j: (0, j))
    return pl.pallas_call(
        body,
        grid=(cols // FC,),
        in_specs=[whole((toks, DS)), whole((toks, DS)), weight_spec(weight, 0, FC)],
        out_specs=[chunk, chunk],
        out_shape=[
            jax.ShapeDtypeStruct((2 * toks, cols), F32),
            jax.ShapeDtypeStruct((2 * toks, cols), BF16),
        ],
        compiler_params=PARAMS,
        cost_estimate=TINY,
        name="forward",
    )(normed_own, normed_pair, weight)


def forward_pieces(normed_own, normed_pair, pieces):
    toks = normed_own.shape[0]
    cols = pieces[0][0].shape[1]
    count = len(pieces)

    def body(offs_ref, no, np_, *refs):
        parts, (pre, act, w, sems) = refs[:count], refs[count:]
        j = pl.program_id(0)

        @pl.when(j == 0)
        def _():
            copies = piece_copies(pieces, offs_ref, parts, w, sems)
            for copy in copies:
                copy.start()
            for copy in copies:
                copy.wait()

        chunk = w[:, pl.ds(pl.multiple_of(j * FC, FC), FC)]
        for part, off in ((no, 0), (np_, toks)):
            value = jnp.dot(part[...], chunk, preferred_element_type=F32)
            pre[off : off + toks, :] = value
            act[off : off + toks, :] = gelu_value(value).astype(BF16)

    chunk = pl.BlockSpec((2 * toks, FC), lambda j: (0, j))
    return pl.pallas_call(
        body,
        grid=(cols // FC,),
        in_specs=[pl.BlockSpec(memory_space=pltpu.SMEM), whole((toks, DS)), whole((toks, DS))]
        + [pl.BlockSpec(memory_space=pl.ANY)] * count,
        out_specs=[chunk, chunk],
        out_shape=[
            jax.ShapeDtypeStruct((2 * toks, cols), F32),
            jax.ShapeDtypeStruct((2 * toks, cols), BF16),
        ],
        scratch_shapes=[pltpu.VMEM((DS, cols), BF16), pltpu.SemaphoreType.DMA((count,))],
        compiler_params=PARAMS,
        cost_estimate=TINY,
        name="forward_far",
    )(piece_offsets(pieces), normed_own, normed_pair, *[p[0] for p in pieces])


def branch_pieces(near, act, pieces, which, dtype):
    toks = act.shape[0] // 2
    cols = act.shape[1]
    step = 2 * FC
    n = cols // step
    count = len(pieces)

    def body(offs_ref, nr, a, *refs):
        parts, (out, acc, w, sems) = refs[:count], refs[count:]
        j = pl.program_id(0)

        @pl.when(j == 0)
        def _():
            copies = piece_copies(pieces, offs_ref, parts, w, sems)
            for copy in copies:
                copy.start()
            acc[...] = nr[...]
            for copy in copies:
                copy.wait()

        acc[...] += nt(a[...], w[:, pl.ds(pl.multiple_of(j * step, step), step)])

        @pl.when(j == n - 1)
        def _():
            out[...] = acc[...].astype(out.dtype)

    return pl.pallas_call(
        body,
        grid=(n,),
        in_specs=[
            pl.BlockSpec(memory_space=pltpu.SMEM),
            pl.BlockSpec((toks, DS), lambda j: (which, 0)),
            pl.BlockSpec((toks, step), lambda j: (which, j)),
        ]
        + [pl.BlockSpec(memory_space=pl.ANY)] * count,
        out_specs=whole((toks, DS)),
        out_shape=jax.ShapeDtypeStruct((toks, DS), dtype),
        scratch_shapes=[
            pltpu.VMEM((toks, DS), F32),
            pltpu.VMEM((DS, cols), BF16),
            pltpu.SemaphoreType.DMA((count,)),
        ],
        compiler_params=PARAMS,
        cost_estimate=TINY,
        name="branch_far",
    )(piece_offsets(pieces), near, act, *[p[0] for p in pieces])


def weight_spec(weight, which, width):
    if weight.ndim == 2:
        return pl.BlockSpec((DS, width), lambda j: (0, j))
    return pl.BlockSpec((4, 1, DS // 4, width), lambda j: (0, which, 0, j))


def flat(w):
    return w[...].reshape(DS, w.shape[-1])


def branch_near_part(act, weight):
    count, cols = act.shape
    step = 2 * FC

    def body(a, w, out):
        value = nt(a[...], flat(w))

        @pl.when(pl.program_id(0) == 0)
        def _():
            out[...] = value

        @pl.when(pl.program_id(0) > 0)
        def _():
            out[...] += value

    return pl.pallas_call(
        body,
        grid=(cols // step,),
        in_specs=[
            pl.BlockSpec((count, step), lambda j: (0, j)),
            weight_spec(weight, 1, step),
        ],
        out_specs=whole((count, DS)),
        out_shape=jax.ShapeDtypeStruct((count, DS), F32),
        compiler_params=PARAMS,
        cost_estimate=TINY,
        name="branch_near",
    )(act, weight)


def branch_part(near, act, weight, which, dtype):
    toks = act.shape[0] // 2
    cols = act.shape[1]
    step = 2 * FC
    n = cols // step

    def body(nr, a, w, out, acc):
        j = pl.program_id(0)

        @pl.when(j == 0)
        def _():
            acc[...] = nr[...]

        acc[...] += nt(a[...], w[...])

        @pl.when(j == n - 1)
        def _():
            out[...] = acc[...].astype(out.dtype)

    return pl.pallas_call(
        body,
        grid=(n,),
        in_specs=[
            pl.BlockSpec((toks, DS), lambda j: (which, 0)),
            pl.BlockSpec((toks, step), lambda j: (which, j)),
            pl.BlockSpec((DS, step), lambda j: (0, j)),
        ],
        out_specs=whole((toks, DS)),
        out_shape=jax.ShapeDtypeStruct((toks, DS), dtype),
        scratch_shapes=[pltpu.VMEM((toks, DS), F32)],
        compiler_params=PARAMS,
        cost_estimate=TINY,
        name="branch",
    )(near, act, weight)


def store_blocks(mx, acc, scratch, outs):
    if len(outs) == 1:
        outs[0][...] = acc.astype(BF16)
        return
    rows = DS // 4
    scratch[...] = acc.astype(BF16)
    for k, out in enumerate(outs):
        off = pl.multiple_of((mx ^ k) * rows, 32)
        out[...] = scratch[pl.ds(off, rows), :]


def block_outs(split, cols):
    count, rows = (4, DS // 4) if split else (1, DS)
    specs = [pl.BlockSpec((rows, FC), lambda j: (0, j))] * count
    shapes = [jax.ShapeDtypeStruct((rows, cols), BF16)] * count
    return specs, shapes


def grad_out_part(mx, grad_own, grad_pair, act, split):
    toks = grad_own.shape[0]
    cols = act.shape[1]
    specs, shapes = block_outs(split, cols)

    def body(mx_ref, go, gp, a, *rest):
        outs, (gt, scratch) = rest[:-2], rest[-2:]

        @pl.when(pl.program_id(0) == 0)
        def _():
            gt[:, :toks] = go[...].T
            gt[:, toks:] = gp[...].T

        acc = jnp.dot(gt[...], a[...], preferred_element_type=F32)
        store_blocks(mx_ref[0], acc, scratch, outs)

    return pl.pallas_call(
        body,
        grid=(cols // FC,),
        in_specs=[
            pl.BlockSpec(memory_space=pltpu.SMEM),
            whole((toks, DS)),
            whole((toks, DS)),
            pl.BlockSpec((2 * toks, FC), lambda j: (0, j)),
        ],
        out_specs=specs,
        out_shape=shapes,
        scratch_shapes=[pltpu.VMEM((DS, 2 * toks), BF16), pltpu.VMEM((DS, FC), BF16)],
        compiler_params=LIGHT,
        cost_estimate=TINY,
        name="grad_out",
    )(mx, grad_own, grad_pair, act)


def grad_in_part(mx, grad_own, grad_pair, w_out, slope, normed_t, split):
    toks = grad_own.shape[0]
    cols = w_out.shape[-1]
    specs, shapes = block_outs(split, cols)

    def body(mx_ref, go, gp, w, sl, nrm, *rest):
        outs, (pre, scratch) = rest[:-2], rest[-2:]
        for part, off in ((go, 0), (gp, toks)):
            act_grad = jnp.dot(part[...], flat(w), preferred_element_type=F32)
            pre[off : off + toks, :] = (act_grad * sl[off : off + toks, :]).astype(BF16)
        acc = jnp.dot(nrm[...], pre[...], preferred_element_type=F32)
        store_blocks(mx_ref[0], acc, scratch, outs)

    return pl.pallas_call(
        body,
        grid=(cols // FC,),
        in_specs=[
            pl.BlockSpec(memory_space=pltpu.SMEM),
            whole((toks, DS)),
            whole((toks, DS)),
            weight_spec(w_out, 1, FC),
            pl.BlockSpec((2 * toks, FC), lambda j: (0, j)),
            whole((DS, 2 * toks)),
        ],
        out_specs=specs,
        out_shape=shapes,
        scratch_shapes=[pltpu.VMEM((2 * toks, FC), BF16), pltpu.VMEM((DS, FC), BF16)],
        compiler_params=LIGHT,
        cost_estimate=TINY,
        name="grad_in",
    )(mx, grad_own, grad_pair, w_out, slope, normed_t)


def after(value, *deps):
    return lax.optimization_barrier((value,) + deps)[0]


def together(*values):
    return lax.optimization_barrier(values)


def nt(left, right):
    return lax.dot_general(left, right, (((1,), (1,)), ((), ())), preferred_element_type=F32)


def tn(left, right):
    return lax.dot_general(
        left, right, (((0,), (0,)), ((), ())), preferred_element_type=F32
    ).astype(BF16)


def pair_shards(teacher_feats, t_gain, t_bias, projection, student_in, s_gain, w_in, w_out):
    mx = lax.axis_index("mx")
    g = lax.axis_index("group")
    patch_all, image_loc, feat_loc = teacher_feats.shape
    patch_loc = patch_all // 4
    toks = patch_loc * image_loc
    tokens = PATCHES * image_loc * 4
    w_out = w_out.T
    rows, cols = w_in.shape
    half = rows // 2
    mine, other = g * half, (1 - g) * half

    mx1 = mx.reshape(1).astype(jnp.int32)

    def my_half(w):
        return lax.dynamic_slice(w, (mine, 0), (half, cols))

    z_send = jnp.concatenate([my_half(w_in), my_half(w_out)], axis=0)
    z_g = swap(z_send, "my", 2)
    near = lax.all_gather(jnp.concatenate([w_in, w_out], axis=0), "mx", axis=0, tiled=True)
    near = near.reshape(4, 2, rows, cols)

    feats = teacher_feats.reshape(4 * toks, feat_loc)
    student = student_in.reshape(toks, DS)
    normed_own = student_norm(after(student, z_send), s_gain.reshape(1, DS))
    normed_pair = swap(normed_own, "my", 1)
    sums = teacher_sums(after(feats, normed_own))
    sums = lax.psum(sums[:2], "mx")
    gain = t_gain.astype(F32).reshape(1, feat_loc)
    bias = t_bias.astype(F32).reshape(1, feat_loc)
    parts = target_parts(mx1, (3, 2, 1, 0), feats, sums, gain, bias, projection)
    q3, q2, q1, q0, z_g, normed_pair = together(*parts, z_g, normed_pair)

    d_g = swap(z_g, "mx", 2)
    z_o = swap(z_g, "group", 1)
    zgc = swap(z_g, "mx", 1)
    q3c = swap(q3, "mx", 1)
    pre_near, act_near = forward_part(normed_own, normed_pair, near)
    pre_near, act_near, d_g, z_o, zgc, q3c = together(pre_near, act_near, d_g, z_o, zgc, q3c)
    in_do = swap(d_g[:half], "group", 1)
    out_do = swap(z_o[half:], "mx", 2)
    zoc, dgc = swap(z_o, "mx", 1), swap(d_g, "mx", 1)
    t2 = (q2.astype(F32) + q3c.astype(F32)).astype(BF16)
    near_share = branch_near_part(after(act_near, t2), near)
    in_do, out_do, zoc, dgc, near_share = together(in_do, out_do, zoc, dgc, near_share)
    in_doc, out_doc = swap(in_do, "mx", 1), swap(out_do, "mx", 1)
    in_doc, out_doc = together(in_doc, out_doc)

    def far_rows(first, d_o, d_oc):
        out = []
        for part, part_c, block, off, at in (
            (z_g, zgc, 0, mine, first),
            (z_o, zoc, 0, other, first),
            (d_g, dgc, 2, mine, first),
            (d_o, d_oc, 2, other, 0),
        ):
            out.append((part, at, half, (mx ^ block) * rows + off))
            out.append((part_c, at, half, (mx ^ block ^ 1) * rows + off))
        return out

    target_x = swap(after(t2, in_doc), "mx", 2)
    q1c = swap(after(q1, in_doc), "mx", 1)
    pre_far, act_far = forward_pieces(normed_own, normed_pair, far_rows(0, in_do, in_doc))
    pre_far, act_far, q1c = together(pre_far, act_far, q1c)
    out_rows = far_rows(half, out_do, out_doc)
    t0 = q0.astype(F32) + q1c.astype(F32)

    branch_pair = branch_pieces(near_share, act_far, out_rows, 1, BF16)
    branch_recv = swap(branch_pair, "my", 1)
    out_far = assemble([(p, at, n, after(o, branch_pair)) for p, at, n, o in out_rows], DS)
    branch_own = branch_part(near_share, act_far, out_far, 0, F32)
    branch_own, target_x = together(branch_own, target_x)
    slope_far = gelu_slope(after(pre_far, branch_own))
    branch_recv = after(branch_recv, slope_far)

    target = t0 + target_x.astype(F32)
    residue = student.astype(F32) + (branch_own + branch_recv.astype(F32)) - target
    grad_own = (residue / jnp.sqrt(jnp.float32(tokens))).astype(BF16)
    loss = jnp.broadcast_to(jnp.sum(residue * residue), (8, 128))
    grad_own, loss = lax.optimization_barrier((grad_own, loss))
    grad_pair = swap(grad_own, "my", 1)
    for bit in (1, 2):
        loss = loss + swap(loss, "mx", bit)
    slope_near = gelu_slope(after(pre_near, grad_own))
    normed_t = jnp.concatenate([after(normed_own, slope_near).T, normed_pair.T], axis=1)
    grad_pair, loss, slope_near, normed_t = together(grad_pair, loss, slope_near, normed_t)

    o0, o1, o2, o3 = grad_out_part(mx1, grad_own, grad_pair, act_far, True)
    got2, got0 = swap(o3, "mx", 1), swap(o1, "mx", 1)
    early = rows // 48 * 16 + 16
    h0, h1 = slice(0, early), slice(early, rows)
    s2_out = [(o2[c].astype(F32) + got2[c].astype(F32)).astype(BF16) for c in (h0, h1)]
    x_out = [swap(v, "mx", 2) for v in s2_out]
    n0, n1, n2, n3 = grad_out_part(mx1, after(grad_own, *s2_out), grad_pair, act_near, True)
    n0, n1, n2, n3, x_out0, got0 = together(n0, n1, n2, n3, x_out[0], got0)

    def last(keep, got, x):
        return (keep.astype(F32) + got.astype(F32) + x.astype(F32)).astype(BF16)

    f0 = last(o0[h0], got0[h0], x_out0)
    f_out0 = swap(f0, "my", 2)
    gn2, gn0 = swap(after(n3, f0), "mx", 1), swap(after(n1, f0), "mx", 1)
    i0, i1, i2, i3 = grad_in_part(
        mx1, after(grad_own, f0), grad_pair, out_far, slope_far, normed_t, True
    )
    i0, i1, i2, i3, x_out1, gn2, gn0, f_out0 = together(
        i0, i1, i2, i3, x_out[1], gn2, gn0, f_out0
    )
    f1 = last(o0[h1], got0[h1], x_out1)
    f_out1, f_out2 = (swap(f1[c], "my", 2) for c in (slice(0, 48), slice(48, None)))
    gin2, gin0 = swap(i3, "mx", 1), swap(i1, "mx", 1)
    loss_z = swap(after(loss, f1), "my", 1)
    s2_on = (n2.astype(F32) + gn2.astype(F32)).astype(BF16)
    gin2, gin0, s2_on, loss_z, f_out1 = together(gin2, gin0, s2_on, loss_z, f_out1)
    loss = loss + loss_z
    s2_in = (i2.astype(F32) + gin2.astype(F32)).astype(BF16)
    x_in = swap(s2_in, "mx", 2)
    x_on = swap(after(s2_on, s2_in), "mx", 2)
    m0, m1, m2, m3 = grad_in_part(
        mx1, after(grad_own, s2_on, s2_in), grad_pair, near, slope_near, normed_t, True
    )
    m0, m1, m2, m3, x_in, f_out2 = together(m0, m1, m2, m3, x_in, f_out2)
    f2 = [last(i0[c], gin0[c], x_in[c]) for c in (h0, h1)]
    f_in = [swap(v, "my", 2) for v in f2]
    gm2, gm0 = swap(after(m3, *f2), "mx", 1), swap(after(m1, *f2), "mx", 1)
    loss_z = swap(after(loss, *f2), "my", 2)
    gm2, gm0, x_on, f_in0, loss_z = together(gm2, gm0, x_on, f_in[0], loss_z)
    mse_loss = (loss + loss_z)[0, :1] / (tokens * DS)
    s2_mn = (m2.astype(F32) + gm2.astype(F32)).astype(BF16)
    x_mn = swap(s2_mn, "mx", 2)
    grad_out_near = n0.astype(F32) + gn0.astype(F32) + x_on.astype(F32)
    grad_in_near = m0.astype(F32) + gm0.astype(F32) + x_mn.astype(F32)
    f_out = jnp.concatenate([f_out0, f_out1, f_out2], axis=0)
    f_in = jnp.concatenate([f_in0, f_in[1]], axis=0)
    grad_out = (grad_out_near + f_out.astype(F32)).T
    grad_in = grad_in_near + f_in.astype(F32)
    return (mse_loss, grad_in, grad_out)


def shards(teacher_feats, t_gain, t_bias, projection, student_in, s_gain, w_in, w_out):
    patch_all, image_loc, feat_loc = teacher_feats.shape
    mx_count = lax.axis_size("mx")
    my_count = lax.axis_size("my")
    patch_loc = patch_all // mx_count
    features = teacher_feats.astype(jnp.float32)
    feature_sum, squares = lax.psum(
        (jnp.sum(features, axis=2), jnp.sum(features * features, axis=2)), "mx"
    )
    row_mean = feature_sum / DT
    variance = squares / DT - row_mean * row_mean
    normed_teacher = (
        (features - row_mean[..., None])
        * lax.rsqrt(variance + epsilon)[..., None]
        * t_gain.astype(jnp.float32)
        + t_bias.astype(jnp.float32)
    ).astype(jnp.bfloat16)
    flattened = normed_teacher.reshape(patch_loc * lax.axis_size("mx") * image_loc, feat_loc)
    target = lax.psum_scatter(
        jnp.dot(flattened, projection, preferred_element_type=jnp.float32)
        .reshape(patch_loc * lax.axis_size("mx"), image_loc, DS)
        .astype(jnp.bfloat16),
        "mx",
        scatter_dimension=0,
        tiled=True,
    ).astype(jnp.float32)
    student_f32 = student_in.astype(jnp.float32)
    student_mean = jnp.sum(student_f32, axis=2, keepdims=True) / DS
    student_square = jnp.sum(student_f32 * student_f32, axis=2, keepdims=True) / DS
    normed = (
        (student_f32 - student_mean)
        * lax.rsqrt(student_square - student_mean * student_mean + epsilon)
        * s_gain
    ).astype(jnp.bfloat16)
    gathered = lax.all_gather(normed, "my", axis=1, tiled=True)
    rows_all = patch_loc * image_loc * my_count
    normed_flat = gathered.reshape(rows_all, DS)
    preact = jnp.dot(
        normed_flat,
        lax.all_gather(w_in, "mx", axis=0, tiled=True),
        preferred_element_type=jnp.float32,
    )
    activation = gelu_value(preact).astype(jnp.bfloat16)
    w_out_full = lax.all_gather(w_out, "mx", axis=1, tiled=True)
    branch_part = jnp.dot(activation, w_out_full, preferred_element_type=jnp.float32).reshape(
        patch_loc, image_loc * my_count, DS
    )
    branch = lax.psum_scatter(
        branch_part.astype(jnp.bfloat16), "my", scatter_dimension=1, tiled=True
    ).astype(jnp.float32)
    residue = student_f32 + branch - target
    tokens = PATCHES * image_loc * my_count
    squared_sum = lax.psum(jnp.sum(residue * residue), ("mx", "my"))
    mse_loss = jnp.reshape(squared_sum / (tokens * DS), (1,))
    grad_output = (residue / jnp.sqrt(jnp.float32(tokens))).astype(jnp.bfloat16)
    grad_rows = lax.all_gather(grad_output, "my", axis=1, tiled=True).reshape(rows_all, DS)
    grad_act = lax.dot_general(
        grad_rows, w_out_full, (((1,), (1,)), ((), ())), preferred_element_type=jnp.float32
    )
    grad_pre = (grad_act * gelu_slope(preact)).astype(jnp.bfloat16)
    part_in = lax.dot_general(
        normed_flat, grad_pre, (((0,), (0,)), ((), ())), preferred_element_type=jnp.float32
    )
    part_out = lax.dot_general(
        activation, grad_rows, (((0,), (0,)), ((), ())), preferred_element_type=jnp.float32
    )
    grad_in = lax.psum_scatter(
        part_in.astype(jnp.bfloat16), "mx", scatter_dimension=0, tiled=True
    ).astype(jnp.float32)
    grad_out = lax.psum_scatter(
        part_out.astype(jnp.bfloat16), "mx", scatter_dimension=1, tiled=True
    ).astype(jnp.float32)
    return (mse_loss, grad_in, grad_out)


def solution(mesh):
    in_specs = (
        P(None, ("group", "my"), "mx"),
        P("mx"),
        P("mx"),
        P("mx", None),
        P("mx", ("group", "my"), None),
        P(),
        P("mx", "my"),
        P("my", "mx"),
    )
    out_specs = (P("group"), P(("group", "mx"), "my"), P(("group", "my"), "mx"))
    pairs = mesh.shape["group"] == 2 and mesh.shape["mx"] == 4 and mesh.shape["my"] == 4
    body = pair_shards if pairs else shards
    return jax.shard_map(body, mesh=mesh, in_specs=in_specs, out_specs=out_specs, check_vma=False)
```

```python
import jax
import jax.numpy as jnp
from jax import lax
from jax.experimental import pallas as pl
from jax.experimental.pallas import tpu as pltpu
from jax.sharding import PartitionSpec as P

DT = 6144
DS = 1408
PATCHES = 256
F32 = jnp.float32
BF16 = jnp.bfloat16

epsilon = 1e-06

FC = 256
TINY = pl.CostEstimate(flops=1000, transcendentals=0, bytes_accessed=1000)
PARAMS = pltpu.CompilerParams(vmem_limit_bytes=58 * 2**20)
LIGHT = pltpu.CompilerParams(vmem_limit_bytes=24 * 2**20)


def gelu_value(value):
    return 0.5 * value * (1.0 + lax.erf(value * 0.7071067811865476))


def gelu_slope(value):
    return (
        0.5 * (1.0 + lax.erf(value * 0.7071067811865476))
        + value * jnp.exp(-0.5 * value * value) * 0.3989422804014327
    )


def swap(value, axis, bit):
    count = lax.axis_size(axis)
    return lax.ppermute(value, axis, [(i, i ^ bit) for i in range(count)])


def piece_copies(pieces, offs_ref, parts, out, sems):
    copies = []
    for i, part in enumerate(parts):
        first, count = pieces[i][1:3]
        off = pl.multiple_of(offs_ref[i], 16)
        copies.append(
            pltpu.make_async_copy(
                part.at[first : first + count, :], out.at[pl.ds(off, count), :], sems.at[i]
            )
        )
    return copies


def piece_offsets(pieces):
    return jnp.stack([jnp.asarray(p[3], jnp.int32) for p in pieces])


def assemble(pieces, rows):
    arrays = [p[0] for p in pieces]
    cols = arrays[0].shape[1]
    offs = piece_offsets(pieces)

    def body(offs_ref, *refs):
        parts, out, sems = refs[:-2], refs[-2], refs[-1]
        copies = piece_copies(pieces, offs_ref, parts, out, sems)
        for copy in copies:
            copy.start()
        for copy in copies:
            copy.wait()

    return pl.pallas_call(
        body,
        out_shape=jax.ShapeDtypeStruct((rows, cols), arrays[0].dtype),
        in_specs=[pl.BlockSpec(memory_space=pltpu.SMEM)]
        + [pl.BlockSpec(memory_space=pl.ANY)] * len(pieces),
        out_specs=pl.BlockSpec(memory_space=pltpu.VMEM),
        scratch_shapes=[pltpu.SemaphoreType.DMA((len(pieces),))],
        cost_estimate=TINY,
        compiler_params=PARAMS,
        name="assemble",
    )(offs, *arrays)


def whole(shape):
    return pl.BlockSpec(shape, lambda j: (0,) * len(shape))


def turned(value):
    part = value[:, :128]
    for at in range(128, value.shape[1], 128):
        part = part + value[:, at : at + 128]
    return jnp.sum(part.T, axis=0, keepdims=True)


def teacher_sums(feats):
    count, width = feats.shape
    step = 512

    def body(x_ref, out):
        x = x_ref[...].astype(F32)
        out[0:1, :] = turned(x)
        out[1:2, :] = turned(x * x)
        out[2:, :] = jnp.zeros((6, step), F32)

    return pl.pallas_call(
        body,
        grid=(count // step,),
        in_specs=[pl.BlockSpec((step, width), lambda j: (j, 0))],
        out_specs=pl.BlockSpec((8, step), lambda j: (0, j)),
        out_shape=jax.ShapeDtypeStruct((8, count), F32),
        compiler_params=PARAMS,
        cost_estimate=TINY,
        name="teacher_sums",
    )(feats)


def target_parts(mx, ks, feats, sums, gain, bias, projection):
    count, width = feats.shape
    step = 256
    toks = count // 4
    per = toks // step

    def body(mx_ref, x_ref, s_ref, g_ref, b_ref, w_ref, *outs):
        j = pl.program_id(0)
        sums_t = jnp.concatenate([s_ref[...], jnp.zeros((6, step), F32)], axis=0).T
        mean = sums_t[:, 0:1] / DT
        rstd = lax.rsqrt(sums_t[:, 1:2] / DT - mean * mean + epsilon)
        tnorm = (x_ref[...].astype(F32) - mean) * rstd * g_ref[...] + b_ref[...]
        value = jnp.dot(tnorm.astype(BF16), w_ref[...], preferred_element_type=F32).astype(BF16)
        for n, out in enumerate(outs):

            @pl.when(j // per == n)
            def _(out=out):
                out[...] = value

    def row(j, mx_ref):
        k = ks[0] - j // per
        return (mx_ref[0] ^ k) * per + j % per

    return pl.pallas_call(
        body,
        grid_spec=pltpu.PrefetchScalarGridSpec(
            num_scalar_prefetch=1,
            grid=(len(ks) * per,),
            in_specs=[
                pl.BlockSpec((step, width), lambda j, m: (row(j, m), 0)),
                pl.BlockSpec((2, step), lambda j, m: (0, row(j, m))),
                pl.BlockSpec((1, width), lambda j, m: (0, 0)),
                pl.BlockSpec((1, width), lambda j, m: (0, 0)),
                pl.BlockSpec((width, DS), lambda j, m: (0, 0)),
            ],
            out_specs=[
                pl.BlockSpec(
                    (step, DS), lambda j, m, n=n: (jnp.clip(j - n * per, 0, per - 1), 0)
                )
                for n in range(len(ks))
            ],
        ),
        out_shape=[jax.ShapeDtypeStruct((toks, DS), BF16)] * len(ks),
        compiler_params=PARAMS,
        cost_estimate=TINY,
        name="targets",
    )(mx, feats, sums, gain, bias, projection)


def student_norm(student, gain):
    count, width = student.shape
    step = 128

    def body(x_ref, g_ref, out):
        x = x_ref[...].astype(F32)
        mean = jnp.sum(x, axis=1, keepdims=True) / DS
        square = jnp.sum(x * x, axis=1, keepdims=True) / DS
        out[...] = ((x - mean) * lax.rsqrt(square - mean * mean + epsilon) * g_ref[...]).astype(BF16)

    return pl.pallas_call(
        body,
        grid=(count // step,),
        in_specs=[
            pl.BlockSpec((step, width), lambda j: (j, 0)),
            pl.BlockSpec((1, width), lambda j: (0, 0)),
        ],
        out_specs=pl.BlockSpec((step, width), lambda j: (j, 0)),
        out_shape=jax.ShapeDtypeStruct((count, width), BF16),
        compiler_params=LIGHT,
        cost_estimate=TINY,
        name="student_norm",
    )(student, gain)


def forward_part(normed_own, normed_pair, weight):
    toks = normed_own.shape[0]
    cols = weight.shape[-1]

    def body(no, np_, w, pre, act):
        for part, off in ((no, 0), (np_, toks)):
            value = jnp.dot(part[...], flat(w), preferred_element_type=F32)
            pre[off : off + toks, :] = value
            act[off : off + toks, :] = gelu_value(value).astype(BF16)

    chunk = pl.BlockSpec((2 * toks, FC), lambda j: (0, j))
    return pl.pallas_call(
        body,
        grid=(cols // FC,),
        in_specs=[whole((toks, DS)), whole((toks, DS)), weight_spec(weight, 0, FC)],
        out_specs=[chunk, chunk],
        out_shape=[
            jax.ShapeDtypeStruct((2 * toks, cols), F32),
            jax.ShapeDtypeStruct((2 * toks, cols), BF16),
        ],
        compiler_params=PARAMS,
        cost_estimate=TINY,
        name="forward",
    )(normed_own, normed_pair, weight)


def forward_pieces(normed_own, normed_pair, pieces):
    toks = normed_own.shape[0]
    cols = pieces[0][0].shape[1]
    count = len(pieces)

    def body(offs_ref, no, np_, *refs):
        parts, (pre, act, w, sems) = refs[:count], refs[count:]
        j = pl.program_id(0)

        @pl.when(j == 0)
        def _():
            copies = piece_copies(pieces, offs_ref, parts, w, sems)
            for copy in copies:
                copy.start()
            for copy in copies:
                copy.wait()

        chunk = w[:, pl.ds(pl.multiple_of(j * FC, FC), FC)]
        for part, off in ((no, 0), (np_, toks)):
            value = jnp.dot(part[...], chunk, preferred_element_type=F32)
            pre[off : off + toks, :] = value
            act[off : off + toks, :] = gelu_value(value).astype(BF16)

    chunk = pl.BlockSpec((2 * toks, FC), lambda j: (0, j))
    return pl.pallas_call(
        body,
        grid=(cols // FC,),
        in_specs=[pl.BlockSpec(memory_space=pltpu.SMEM), whole((toks, DS)), whole((toks, DS))]
        + [pl.BlockSpec(memory_space=pl.ANY)] * count,
        out_specs=[chunk, chunk],
        out_shape=[
            jax.ShapeDtypeStruct((2 * toks, cols), F32),
            jax.ShapeDtypeStruct((2 * toks, cols), BF16),
        ],
        scratch_shapes=[pltpu.VMEM((DS, cols), BF16), pltpu.SemaphoreType.DMA((count,))],
        compiler_params=PARAMS,
        cost_estimate=TINY,
        name="forward_far",
    )(piece_offsets(pieces), normed_own, normed_pair, *[p[0] for p in pieces])


def branch_pieces(near, act, pieces, which, dtype):
    toks = act.shape[0] // 2
    cols = act.shape[1]
    step = 2 * FC
    n = cols // step
    count = len(pieces)

    def body(offs_ref, nr, a, *refs):
        parts, (out, acc, w, sems) = refs[:count], refs[count:]
        j = pl.program_id(0)

        @pl.when(j == 0)
        def _():
            copies = piece_copies(pieces, offs_ref, parts, w, sems)
            for copy in copies:
                copy.start()
            acc[...] = nr[...]
            for copy in copies:
                copy.wait()

        acc[...] += nt(a[...], w[:, pl.ds(pl.multiple_of(j * step, step), step)])

        @pl.when(j == n - 1)
        def _():
            out[...] = acc[...].astype(out.dtype)

    return pl.pallas_call(
        body,
        grid=(n,),
        in_specs=[
            pl.BlockSpec(memory_space=pltpu.SMEM),
            pl.BlockSpec((toks, DS), lambda j: (which, 0)),
            pl.BlockSpec((toks, step), lambda j: (which, j)),
        ]
        + [pl.BlockSpec(memory_space=pl.ANY)] * count,
        out_specs=whole((toks, DS)),
        out_shape=jax.ShapeDtypeStruct((toks, DS), dtype),
        scratch_shapes=[
            pltpu.VMEM((toks, DS), F32),
            pltpu.VMEM((DS, cols), BF16),
            pltpu.SemaphoreType.DMA((count,)),
        ],
        compiler_params=PARAMS,
        cost_estimate=TINY,
        name="branch_far",
    )(piece_offsets(pieces), near, act, *[p[0] for p in pieces])


def weight_spec(weight, which, width):
    if weight.ndim == 2:
        return pl.BlockSpec((DS, width), lambda j: (0, j))
    return pl.BlockSpec((4, 1, DS // 4, width), lambda j: (0, which, 0, j))


def flat(w):
    return w[...].reshape(DS, w.shape[-1])


def branch_near_part(act, weight):
    count, cols = act.shape
    step = 2 * FC

    def body(a, w, out):
        value = nt(a[...], flat(w))

        @pl.when(pl.program_id(0) == 0)
        def _():
            out[...] = value

        @pl.when(pl.program_id(0) > 0)
        def _():
            out[...] += value

    return pl.pallas_call(
        body,
        grid=(cols // step,),
        in_specs=[
            pl.BlockSpec((count, step), lambda j: (0, j)),
            weight_spec(weight, 1, step),
        ],
        out_specs=whole((count, DS)),
        out_shape=jax.ShapeDtypeStruct((count, DS), F32),
        compiler_params=PARAMS,
        cost_estimate=TINY,
        name="branch_near",
    )(act, weight)


def branch_part(near, act, weight, which, dtype):
    toks = act.shape[0] // 2
    cols = act.shape[1]
    step = 2 * FC
    n = cols // step

    def body(nr, a, w, out, acc):
        j = pl.program_id(0)

        @pl.when(j == 0)
        def _():
            acc[...] = nr[...]

        acc[...] += nt(a[...], w[...])

        @pl.when(j == n - 1)
        def _():
            out[...] = acc[...].astype(out.dtype)

    return pl.pallas_call(
        body,
        grid=(n,),
        in_specs=[
            pl.BlockSpec((toks, DS), lambda j: (which, 0)),
            pl.BlockSpec((toks, step), lambda j: (which, j)),
            pl.BlockSpec((DS, step), lambda j: (0, j)),
        ],
        out_specs=whole((toks, DS)),
        out_shape=jax.ShapeDtypeStruct((toks, DS), dtype),
        scratch_shapes=[pltpu.VMEM((toks, DS), F32)],
        compiler_params=PARAMS,
        cost_estimate=TINY,
        name="branch",
    )(near, act, weight)


def store_blocks(mx, acc, scratch, outs):
    if len(outs) == 1:
        outs[0][...] = acc.astype(BF16)
        return
    rows = DS // 4
    scratch[...] = acc.astype(BF16)
    for k, out in enumerate(outs):
        off = pl.multiple_of((mx ^ k) * rows, 32)
        out[...] = scratch[pl.ds(off, rows), :]


def block_outs(split, cols):
    count, rows = (4, DS // 4) if split else (1, DS)
    specs = [pl.BlockSpec((rows, FC), lambda j: (0, j))] * count
    shapes = [jax.ShapeDtypeStruct((rows, cols), BF16)] * count
    return specs, shapes


def grad_out_part(mx, grad_own, grad_pair, act, split):
    toks = grad_own.shape[0]
    cols = act.shape[1]
    specs, shapes = block_outs(split, cols)

    def body(mx_ref, go, gp, a, *rest):
        outs, (gt, scratch) = rest[:-2], rest[-2:]

        @pl.when(pl.program_id(0) == 0)
        def _():
            gt[:, :toks] = go[...].T
            gt[:, toks:] = gp[...].T

        acc = jnp.dot(gt[...], a[...], preferred_element_type=F32)
        store_blocks(mx_ref[0], acc, scratch, outs)

    return pl.pallas_call(
        body,
        grid=(cols // FC,),
        in_specs=[
            pl.BlockSpec(memory_space=pltpu.SMEM),
            whole((toks, DS)),
            whole((toks, DS)),
            pl.BlockSpec((2 * toks, FC), lambda j: (0, j)),
        ],
        out_specs=specs,
        out_shape=shapes,
        scratch_shapes=[pltpu.VMEM((DS, 2 * toks), BF16), pltpu.VMEM((DS, FC), BF16)],
        compiler_params=LIGHT,
        cost_estimate=TINY,
        name="grad_out",
    )(mx, grad_own, grad_pair, act)


def grad_in_part(mx, grad_own, grad_pair, w_out, slope, normed_t, split):
    toks = grad_own.shape[0]
    cols = w_out.shape[-1]
    specs, shapes = block_outs(split, cols)

    def body(mx_ref, go, gp, w, sl, nrm, *rest):
        outs, (pre, scratch) = rest[:-2], rest[-2:]
        for part, off in ((go, 0), (gp, toks)):
            act_grad = jnp.dot(part[...], flat(w), preferred_element_type=F32)
            pre[off : off + toks, :] = (act_grad * sl[off : off + toks, :]).astype(BF16)
        acc = jnp.dot(nrm[...], pre[...], preferred_element_type=F32)
        store_blocks(mx_ref[0], acc, scratch, outs)

    return pl.pallas_call(
        body,
        grid=(cols // FC,),
        in_specs=[
            pl.BlockSpec(memory_space=pltpu.SMEM),
            whole((toks, DS)),
            whole((toks, DS)),
            weight_spec(w_out, 1, FC),
            pl.BlockSpec((2 * toks, FC), lambda j: (0, j)),
            whole((DS, 2 * toks)),
        ],
        out_specs=specs,
        out_shape=shapes,
        scratch_shapes=[pltpu.VMEM((2 * toks, FC), BF16), pltpu.VMEM((DS, FC), BF16)],
        compiler_params=LIGHT,
        cost_estimate=TINY,
        name="grad_in",
    )(mx, grad_own, grad_pair, w_out, slope, normed_t)


def after(value, *deps):
    return lax.optimization_barrier((value,) + deps)[0]


def together(*values):
    return lax.optimization_barrier(values)


def nt(left, right):
    return lax.dot_general(left, right, (((1,), (1,)), ((), ())), preferred_element_type=F32)


def tn(left, right):
    return lax.dot_general(
        left, right, (((0,), (0,)), ((), ())), preferred_element_type=F32
    ).astype(BF16)


def pair_shards(teacher_feats, t_gain, t_bias, projection, student_in, s_gain, w_in, w_out):
    mx = lax.axis_index("mx")
    g = lax.axis_index("group")
    patch_all, image_loc, feat_loc = teacher_feats.shape
    patch_loc = patch_all // 4
    toks = patch_loc * image_loc
    tokens = PATCHES * image_loc * 4
    w_out = w_out.T
    rows, cols = w_in.shape
    half = rows // 2
    mine, other = g * half, (1 - g) * half

    mx1 = mx.reshape(1).astype(jnp.int32)

    def my_half(w):
        return lax.dynamic_slice(w, (mine, 0), (half, cols))

    z_send = jnp.concatenate([my_half(w_in), my_half(w_out)], axis=0)
    z_g = swap(z_send, "my", 2)
    near = lax.all_gather(jnp.concatenate([w_in, w_out], axis=0), "mx", axis=0, tiled=True)
    near = near.reshape(4, 2, rows, cols)

    feats = teacher_feats.reshape(4 * toks, feat_loc)
    student = student_in.reshape(toks, DS)
    normed_own = student_norm(after(student, z_send), s_gain.reshape(1, DS))
    normed_pair = swap(normed_own, "my", 1)
    sums = teacher_sums(after(feats, normed_own))
    sums = lax.psum(sums[:2], "mx")
    gain = t_gain.astype(F32).reshape(1, feat_loc)
    bias = t_bias.astype(F32).reshape(1, feat_loc)
    parts = target_parts(mx1, (3, 2, 1, 0), feats, sums, gain, bias, projection)
    q3, q2, q1, q0, z_g, normed_pair = together(*parts, z_g, normed_pair)

    d_g = swap(z_g, "mx", 2)
    z_o = swap(z_g, "group", 1)
    zgc = swap(z_g, "mx", 1)
    q3c = swap(q3, "mx", 1)
    pre_near, act_near = forward_part(normed_own, normed_pair, near)
    near_share = branch_near_part(act_near, near)
    pre_near, act_near, near_share, d_g, z_o, zgc, q3c = together(
        pre_near, act_near, near_share, d_g, z_o, zgc, q3c
    )
    in_do = swap(d_g[:half], "group", 1)
    out_do = swap(z_o[half:], "mx", 2)
    zoc, dgc = swap(z_o, "mx", 1), swap(d_g, "mx", 1)
    t2 = (q2.astype(F32) + q3c.astype(F32)).astype(BF16)
    in_do, out_do, zoc, dgc, t2 = together(in_do, out_do, zoc, dgc, t2)
    in_doc, out_doc = swap(in_do, "mx", 1), swap(out_do, "mx", 1)
    in_doc, out_doc = together(in_doc, out_doc)

    def far_rows(first, d_o, d_oc):
        out = []
        for part, part_c, block, off, at in (
            (z_g, zgc, 0, mine, first),
            (z_o, zoc, 0, other, first),
            (d_g, dgc, 2, mine, first),
            (d_o, d_oc, 2, other, 0),
        ):
            out.append((part, at, half, (mx ^ block) * rows + off))
            out.append((part_c, at, half, (mx ^ block ^ 1) * rows + off))
        return out

    target_x = swap(after(t2, in_doc), "mx", 2)
    q1c = swap(after(q1, in_doc), "mx", 1)
    pre_far, act_far = forward_pieces(normed_own, normed_pair, far_rows(0, in_do, in_doc))
    pre_far, act_far, q1c = together(pre_far, act_far, q1c)
    out_rows = far_rows(half, out_do, out_doc)
    t0 = q0.astype(F32) + q1c.astype(F32)

    branch_pair = branch_pieces(near_share, act_far, out_rows, 1, BF16)
    branch_recv = swap(branch_pair, "my", 1)
    out_far = assemble([(p, at, n, after(o, branch_pair)) for p, at, n, o in out_rows], DS)
    branch_own = branch_part(near_share, act_far, out_far, 0, F32)
    branch_own, target_x = together(branch_own, target_x)
    slope_far = gelu_slope(after(pre_far, branch_own))
    branch_recv = after(branch_recv, slope_far)

    target = t0 + target_x.astype(F32)
    residue = student.astype(F32) + (branch_own + branch_recv.astype(F32)) - target
    grad_own = (residue / jnp.sqrt(jnp.float32(tokens))).astype(BF16)
    loss = jnp.broadcast_to(jnp.sum(residue * residue), (8, 128))
    grad_own, loss = lax.optimization_barrier((grad_own, loss))
    grad_pair = swap(grad_own, "my", 1)
    for bit in (1, 2):
        loss = loss + swap(loss, "mx", bit)
    slope_near = gelu_slope(after(pre_near, grad_own))
    normed_t = jnp.concatenate([after(normed_own, slope_near).T, normed_pair.T], axis=1)
    grad_pair, loss, slope_near, normed_t = together(grad_pair, loss, slope_near, normed_t)

    o0, o1, o2, o3 = grad_out_part(mx1, grad_own, grad_pair, act_far, True)
    got2, got0 = swap(o3, "mx", 1), swap(o1, "mx", 1)
    early = rows // 48 * 16 + 16
    h0, h1 = slice(0, early), slice(early, rows)
    s2_out = [(o2[c].astype(F32) + got2[c].astype(F32)).astype(BF16) for c in (h0, h1)]
    x_out = [swap(v, "mx", 2) for v in s2_out]
    n0, n1, n2, n3 = grad_out_part(mx1, after(grad_own, *s2_out), grad_pair, act_near, True)
    n0, n1, n2, n3, x_out0, got0 = together(n0, n1, n2, n3, x_out[0], got0)

    def last(keep, got, x):
        return (keep.astype(F32) + got.astype(F32) + x.astype(F32)).astype(BF16)

    f0 = last(o0[h0], got0[h0], x_out0)
    f_out0 = swap(f0, "my", 2)
    gn2, gn0 = swap(after(n3, f0), "mx", 1), swap(after(n1, f0), "mx", 1)
    i0, i1, i2, i3 = grad_in_part(
        mx1, after(grad_own, f0), grad_pair, out_far, slope_far, normed_t, True
    )
    i0, i1, i2, i3, x_out1, gn2, gn0, f_out0 = together(
        i0, i1, i2, i3, x_out[1], gn2, gn0, f_out0
    )
    f1 = last(o0[h1], got0[h1], x_out1)
    f_out1, f_out2 = (swap(f1[c], "my", 2) for c in (slice(0, 48), slice(48, None)))
    gin2, gin0 = swap(i3, "mx", 1), swap(i1, "mx", 1)
    loss_z = swap(after(loss, f1), "my", 1)
    s2_on = (n2.astype(F32) + gn2.astype(F32)).astype(BF16)
    gin2, gin0, s2_on, loss_z, f_out1 = together(gin2, gin0, s2_on, loss_z, f_out1)
    loss = loss + loss_z
    s2_in = (i2.astype(F32) + gin2.astype(F32)).astype(BF16)
    x_in = swap(s2_in, "mx", 2)
    x_on = swap(after(s2_on, s2_in), "mx", 2)
    m0, m1, m2, m3 = grad_in_part(
        mx1, after(grad_own, s2_on, s2_in), grad_pair, near, slope_near, normed_t, True
    )
    m0, m1, m2, m3, x_in, f_out2 = together(m0, m1, m2, m3, x_in, f_out2)
    f2 = [last(i0[c], gin0[c], x_in[c]) for c in (h0, h1)]
    f_in = [swap(v, "my", 2) for v in f2]
    gm2, gm0 = swap(after(m3, *f2), "mx", 1), swap(after(m1, *f2), "mx", 1)
    loss_z = swap(after(loss, *f2), "my", 2)
    gm2, gm0, x_on, f_in0, loss_z = together(gm2, gm0, x_on, f_in[0], loss_z)
    mse_loss = (loss + loss_z)[0, :1] / (tokens * DS)
    s2_mn = (m2.astype(F32) + gm2.astype(F32)).astype(BF16)
    x_mn = swap(s2_mn, "mx", 2)
    grad_out_near = n0.astype(F32) + gn0.astype(F32) + x_on.astype(F32)
    grad_in_near = m0.astype(F32) + gm0.astype(F32) + x_mn.astype(F32)
    f_out = jnp.concatenate([f_out0, f_out1, f_out2], axis=0)
    f_in = jnp.concatenate([f_in0, f_in[1]], axis=0)
    grad_out = (grad_out_near + f_out.astype(F32)).T
    grad_in = grad_in_near + f_in.astype(F32)
    return (mse_loss, grad_in, grad_out)


def shards(teacher_feats, t_gain, t_bias, projection, student_in, s_gain, w_in, w_out):
    patch_all, image_loc, feat_loc = teacher_feats.shape
    mx_count = lax.axis_size("mx")
    my_count = lax.axis_size("my")
    patch_loc = patch_all // mx_count
    features = teacher_feats.astype(jnp.float32)
    feature_sum, squares = lax.psum(
        (jnp.sum(features, axis=2), jnp.sum(features * features, axis=2)), "mx"
    )
    row_mean = feature_sum / DT
    variance = squares / DT - row_mean * row_mean
    normed_teacher = (
        (features - row_mean[..., None])
        * lax.rsqrt(variance + epsilon)[..., None]
        * t_gain.astype(jnp.float32)
        + t_bias.astype(jnp.float32)
    ).astype(jnp.bfloat16)
    flattened = normed_teacher.reshape(patch_loc * lax.axis_size("mx") * image_loc, feat_loc)
    target = lax.psum_scatter(
        jnp.dot(flattened, projection, preferred_element_type=jnp.float32)
        .reshape(patch_loc * lax.axis_size("mx"), image_loc, DS)
        .astype(jnp.bfloat16),
        "mx",
        scatter_dimension=0,
        tiled=True,
    ).astype(jnp.float32)
    student_f32 = student_in.astype(jnp.float32)
    student_mean = jnp.sum(student_f32, axis=2, keepdims=True) / DS
    student_square = jnp.sum(student_f32 * student_f32, axis=2, keepdims=True) / DS
    normed = (
        (student_f32 - student_mean)
        * lax.rsqrt(student_square - student_mean * student_mean + epsilon)
        * s_gain
    ).astype(jnp.bfloat16)
    gathered = lax.all_gather(normed, "my", axis=1, tiled=True)
    rows_all = patch_loc * image_loc * my_count
    normed_flat = gathered.reshape(rows_all, DS)
    preact = jnp.dot(
        normed_flat,
        lax.all_gather(w_in, "mx", axis=0, tiled=True),
        preferred_element_type=jnp.float32,
    )
    activation = gelu_value(preact).astype(jnp.bfloat16)
    w_out_full = lax.all_gather(w_out, "mx", axis=1, tiled=True)
    branch_part = jnp.dot(activation, w_out_full, preferred_element_type=jnp.float32).reshape(
        patch_loc, image_loc * my_count, DS
    )
    branch = lax.psum_scatter(
        branch_part.astype(jnp.bfloat16), "my", scatter_dimension=1, tiled=True
    ).astype(jnp.float32)
    residue = student_f32 + branch - target
    tokens = PATCHES * image_loc * my_count
    squared_sum = lax.psum(jnp.sum(residue * residue), ("mx", "my"))
    mse_loss = jnp.reshape(squared_sum / (tokens * DS), (1,))
    grad_output = (residue / jnp.sqrt(jnp.float32(tokens))).astype(jnp.bfloat16)
    grad_rows = lax.all_gather(grad_output, "my", axis=1, tiled=True).reshape(rows_all, DS)
    grad_act = lax.dot_general(
        grad_rows, w_out_full, (((1,), (1,)), ((), ())), preferred_element_type=jnp.float32
    )
    grad_pre = (grad_act * gelu_slope(preact)).astype(jnp.bfloat16)
    part_in = lax.dot_general(
        normed_flat, grad_pre, (((0,), (0,)), ((), ())), preferred_element_type=jnp.float32
    )
    part_out = lax.dot_general(
        activation, grad_rows, (((0,), (0,)), ((), ())), preferred_element_type=jnp.float32
    )
    grad_in = lax.psum_scatter(
        part_in.astype(jnp.bfloat16), "mx", scatter_dimension=0, tiled=True
    ).astype(jnp.float32)
    grad_out = lax.psum_scatter(
        part_out.astype(jnp.bfloat16), "mx", scatter_dimension=1, tiled=True
    ).astype(jnp.float32)
    return (mse_loss, grad_in, grad_out)


def solution(mesh):
    in_specs = (
        P(None, ("group", "my"), "mx"),
        P("mx"),
        P("mx"),
        P("mx", None),
        P("mx", ("group", "my"), None),
        P(),
        P("mx", "my"),
        P("my", "mx"),
    )
    out_specs = (P("group"), P(("group", "mx"), "my"), P(("group", "my"), "mx"))
    pairs = mesh.shape["group"] == 2 and mesh.shape["mx"] == 4 and mesh.shape["my"] == 4
    body = pair_shards if pairs else shards
    return jax.shard_map(body, mesh=mesh, in_specs=in_specs, out_specs=out_specs, check_vma=False)
```

```python
import jax
import jax.numpy as jnp
from jax import lax
from jax.experimental import pallas as pl
from jax.experimental.pallas import tpu as pltpu
from jax.sharding import PartitionSpec as P

DT = 6144
DS = 1408
PATCHES = 256
F32 = jnp.float32
BF16 = jnp.bfloat16

epsilon = 1e-06

FC = 256
TINY = pl.CostEstimate(flops=1000, transcendentals=0, bytes_accessed=1000)
PARAMS = pltpu.CompilerParams(vmem_limit_bytes=58 * 2**20)
LIGHT = pltpu.CompilerParams(vmem_limit_bytes=24 * 2**20)


def gelu_value(value):
    return 0.5 * value * (1.0 + lax.erf(value * 0.7071067811865476))


def gelu_slope(value):
    return (
        0.5 * (1.0 + lax.erf(value * 0.7071067811865476))
        + value * jnp.exp(-0.5 * value * value) * 0.3989422804014327
    )


def swap(value, axis, bit):
    count = lax.axis_size(axis)
    return lax.ppermute(value, axis, [(i, i ^ bit) for i in range(count)])


def piece_copies(pieces, offs_ref, parts, out, sems):
    copies = []
    for i, part in enumerate(parts):
        first, count = pieces[i][1:3]
        off = pl.multiple_of(offs_ref[i], 16)
        copies.append(
            pltpu.make_async_copy(
                part.at[first : first + count, :], out.at[pl.ds(off, count), :], sems.at[i]
            )
        )
    return copies


def piece_offsets(pieces):
    return jnp.stack([jnp.asarray(p[3], jnp.int32) for p in pieces])


def assemble(pieces, rows):
    arrays = [p[0] for p in pieces]
    cols = arrays[0].shape[1]
    offs = piece_offsets(pieces)

    def body(offs_ref, *refs):
        parts, out, sems = refs[:-2], refs[-2], refs[-1]
        copies = piece_copies(pieces, offs_ref, parts, out, sems)
        for copy in copies:
            copy.start()
        for copy in copies:
            copy.wait()

    return pl.pallas_call(
        body,
        out_shape=jax.ShapeDtypeStruct((rows, cols), arrays[0].dtype),
        in_specs=[pl.BlockSpec(memory_space=pltpu.SMEM)]
        + [pl.BlockSpec(memory_space=pl.ANY)] * len(pieces),
        out_specs=pl.BlockSpec(memory_space=pltpu.VMEM),
        scratch_shapes=[pltpu.SemaphoreType.DMA((len(pieces),))],
        cost_estimate=TINY,
        compiler_params=PARAMS,
        name="assemble",
    )(offs, *arrays)


def whole(shape):
    return pl.BlockSpec(shape, lambda j: (0,) * len(shape))


def turned(value):
    part = value[:, :128]
    for at in range(128, value.shape[1], 128):
        part = part + value[:, at : at + 128]
    return jnp.sum(part.T, axis=0, keepdims=True)


def teacher_sums(feats):
    count, width = feats.shape
    step = 512

    def body(x_ref, out):
        x = x_ref[...].astype(F32)
        out[0:1, :] = turned(x)
        out[1:2, :] = turned(x * x)
        out[2:, :] = jnp.zeros((6, step), F32)

    return pl.pallas_call(
        body,
        grid=(count // step,),
        in_specs=[pl.BlockSpec((step, width), lambda j: (j, 0))],
        out_specs=pl.BlockSpec((8, step), lambda j: (0, j)),
        out_shape=jax.ShapeDtypeStruct((8, count), F32),
        compiler_params=PARAMS,
        cost_estimate=TINY,
        name="teacher_sums",
    )(feats)


def target_parts(mx, ks, feats, sums, gain, bias, projection):
    count, width = feats.shape
    step = 256
    toks = count // 4
    per = toks // step

    def body(mx_ref, x_ref, s_ref, g_ref, b_ref, w_ref, *outs):
        j = pl.program_id(0)
        sums_t = jnp.concatenate([s_ref[...], jnp.zeros((6, step), F32)], axis=0).T
        mean = sums_t[:, 0:1] / DT
        rstd = lax.rsqrt(sums_t[:, 1:2] / DT - mean * mean + epsilon)
        tnorm = (x_ref[...].astype(F32) - mean) * rstd * g_ref[...] + b_ref[...]
        value = jnp.dot(tnorm.astype(BF16), w_ref[...], preferred_element_type=F32).astype(BF16)
        for n, out in enumerate(outs):

            @pl.when(j // per == n)
            def _(out=out):
                out[...] = value

    def row(j, mx_ref):
        k = ks[0] - j // per
        return (mx_ref[0] ^ k) * per + j % per

    return pl.pallas_call(
        body,
        grid_spec=pltpu.PrefetchScalarGridSpec(
            num_scalar_prefetch=1,
            grid=(len(ks) * per,),
            in_specs=[
                pl.BlockSpec((step, width), lambda j, m: (row(j, m), 0)),
                pl.BlockSpec((2, step), lambda j, m: (0, row(j, m))),
                pl.BlockSpec((1, width), lambda j, m: (0, 0)),
                pl.BlockSpec((1, width), lambda j, m: (0, 0)),
                pl.BlockSpec((width, DS), lambda j, m: (0, 0)),
            ],
            out_specs=[
                pl.BlockSpec(
                    (step, DS), lambda j, m, n=n: (jnp.clip(j - n * per, 0, per - 1), 0)
                )
                for n in range(len(ks))
            ],
        ),
        out_shape=[jax.ShapeDtypeStruct((toks, DS), BF16)] * len(ks),
        compiler_params=PARAMS,
        cost_estimate=TINY,
        name="targets",
    )(mx, feats, sums, gain, bias, projection)


def student_norm(student, gain):
    count, width = student.shape
    step = 128

    def body(x_ref, g_ref, out):
        x = x_ref[...].astype(F32)
        mean = jnp.sum(x, axis=1, keepdims=True) / DS
        square = jnp.sum(x * x, axis=1, keepdims=True) / DS
        out[...] = ((x - mean) * lax.rsqrt(square - mean * mean + epsilon) * g_ref[...]).astype(BF16)

    return pl.pallas_call(
        body,
        grid=(count // step,),
        in_specs=[
            pl.BlockSpec((step, width), lambda j: (j, 0)),
            pl.BlockSpec((1, width), lambda j: (0, 0)),
        ],
        out_specs=pl.BlockSpec((step, width), lambda j: (j, 0)),
        out_shape=jax.ShapeDtypeStruct((count, width), BF16),
        compiler_params=LIGHT,
        cost_estimate=TINY,
        name="student_norm",
    )(student, gain)


def forward_part(normed_own, normed_pair, weight):
    toks = normed_own.shape[0]
    cols = weight.shape[-1]

    def body(no, np_, w, pre, act):
        for part, off in ((no, 0), (np_, toks)):
            value = jnp.dot(part[...], flat(w), preferred_element_type=F32)
            pre[off : off + toks, :] = value
            act[off : off + toks, :] = gelu_value(value).astype(BF16)

    chunk = pl.BlockSpec((2 * toks, FC), lambda j: (0, j))
    return pl.pallas_call(
        body,
        grid=(cols // FC,),
        in_specs=[whole((toks, DS)), whole((toks, DS)), weight_spec(weight, 0, FC)],
        out_specs=[chunk, chunk],
        out_shape=[
            jax.ShapeDtypeStruct((2 * toks, cols), F32),
            jax.ShapeDtypeStruct((2 * toks, cols), BF16),
        ],
        compiler_params=PARAMS,
        cost_estimate=TINY,
        name="forward",
    )(normed_own, normed_pair, weight)


def forward_pieces(normed_own, normed_pair, pieces):
    toks = normed_own.shape[0]
    cols = pieces[0][0].shape[1]
    count = len(pieces)

    def body(offs_ref, no, np_, *refs):
        parts, (pre, act, w, sems) = refs[:count], refs[count:]
        j = pl.program_id(0)

        @pl.when(j == 0)
        def _():
            copies = piece_copies(pieces, offs_ref, parts, w, sems)
            for copy in copies:
                copy.start()
            for copy in copies:
                copy.wait()

        chunk = w[:, pl.ds(pl.multiple_of(j * FC, FC), FC)]
        for part, off in ((no, 0), (np_, toks)):
            value = jnp.dot(part[...], chunk, preferred_element_type=F32)
            pre[off : off + toks, :] = value
            act[off : off + toks, :] = gelu_value(value).astype(BF16)

    chunk = pl.BlockSpec((2 * toks, FC), lambda j: (0, j))
    return pl.pallas_call(
        body,
        grid=(cols // FC,),
        in_specs=[pl.BlockSpec(memory_space=pltpu.SMEM), whole((toks, DS)), whole((toks, DS))]
        + [pl.BlockSpec(memory_space=pl.ANY)] * count,
        out_specs=[chunk, chunk],
        out_shape=[
            jax.ShapeDtypeStruct((2 * toks, cols), F32),
            jax.ShapeDtypeStruct((2 * toks, cols), BF16),
        ],
        scratch_shapes=[pltpu.VMEM((DS, cols), BF16), pltpu.SemaphoreType.DMA((count,))],
        compiler_params=PARAMS,
        cost_estimate=TINY,
        name="forward_far",
    )(piece_offsets(pieces), normed_own, normed_pair, *[p[0] for p in pieces])


def branch_pieces(near, act, pieces, which, dtype):
    toks = act.shape[0] // 2
    cols = act.shape[1]
    step = 2 * FC
    n = cols // step
    count = len(pieces)

    def body(offs_ref, nr, a, *refs):
        parts, (out, acc, w, sems) = refs[:count], refs[count:]
        j = pl.program_id(0)

        @pl.when(j == 0)
        def _():
            copies = piece_copies(pieces, offs_ref, parts, w, sems)
            for copy in copies:
                copy.start()
            acc[...] = nr[...]
            for copy in copies:
                copy.wait()

        acc[...] += nt(a[...], w[:, pl.ds(pl.multiple_of(j * step, step), step)])

        @pl.when(j == n - 1)
        def _():
            out[...] = acc[...].astype(out.dtype)

    return pl.pallas_call(
        body,
        grid=(n,),
        in_specs=[
            pl.BlockSpec(memory_space=pltpu.SMEM),
            pl.BlockSpec((toks, DS), lambda j: (which, 0)),
            pl.BlockSpec((toks, step), lambda j: (which, j)),
        ]
        + [pl.BlockSpec(memory_space=pl.ANY)] * count,
        out_specs=whole((toks, DS)),
        out_shape=jax.ShapeDtypeStruct((toks, DS), dtype),
        scratch_shapes=[
            pltpu.VMEM((toks, DS), F32),
            pltpu.VMEM((DS, cols), BF16),
            pltpu.SemaphoreType.DMA((count,)),
        ],
        compiler_params=PARAMS,
        cost_estimate=TINY,
        name="branch_far",
    )(piece_offsets(pieces), near, act, *[p[0] for p in pieces])


def weight_spec(weight, which, width):
    if weight.ndim == 2:
        return pl.BlockSpec((DS, width), lambda j: (0, j))
    return pl.BlockSpec((4, 1, DS // 4, width), lambda j: (0, which, 0, j))


def flat(w):
    return w[...].reshape(DS, w.shape[-1])


def branch_near_part(act, weight):
    count, cols = act.shape
    step = 2 * FC

    def body(a, w, out):
        value = nt(a[...], flat(w))

        @pl.when(pl.program_id(0) == 0)
        def _():
            out[...] = value

        @pl.when(pl.program_id(0) > 0)
        def _():
            out[...] += value

    return pl.pallas_call(
        body,
        grid=(cols // step,),
        in_specs=[
            pl.BlockSpec((count, step), lambda j: (0, j)),
            weight_spec(weight, 1, step),
        ],
        out_specs=whole((count, DS)),
        out_shape=jax.ShapeDtypeStruct((count, DS), F32),
        compiler_params=PARAMS,
        cost_estimate=TINY,
        name="branch_near",
    )(act, weight)


def branch_part(near, act, weight, which, dtype):
    toks = act.shape[0] // 2
    cols = act.shape[1]
    step = 2 * FC
    n = cols // step

    def body(nr, a, w, out, acc):
        j = pl.program_id(0)

        @pl.when(j == 0)
        def _():
            acc[...] = nr[...]

        acc[...] += nt(a[...], w[...])

        @pl.when(j == n - 1)
        def _():
            out[...] = acc[...].astype(out.dtype)

    return pl.pallas_call(
        body,
        grid=(n,),
        in_specs=[
            pl.BlockSpec((toks, DS), lambda j: (which, 0)),
            pl.BlockSpec((toks, step), lambda j: (which, j)),
            pl.BlockSpec((DS, step), lambda j: (0, j)),
        ],
        out_specs=whole((toks, DS)),
        out_shape=jax.ShapeDtypeStruct((toks, DS), dtype),
        scratch_shapes=[pltpu.VMEM((toks, DS), F32)],
        compiler_params=PARAMS,
        cost_estimate=TINY,
        name="branch",
    )(near, act, weight)


def store_blocks(mx, acc, scratch, outs):
    if len(outs) == 1:
        outs[0][...] = acc.astype(BF16)
        return
    rows = DS // 4
    scratch[...] = acc.astype(BF16)
    for k, out in enumerate(outs):
        off = pl.multiple_of((mx ^ k) * rows, 32)
        out[...] = scratch[pl.ds(off, rows), :]


def block_outs(split, cols):
    count, rows = (4, DS // 4) if split else (1, DS)
    specs = [pl.BlockSpec((rows, FC), lambda j: (0, j))] * count
    shapes = [jax.ShapeDtypeStruct((rows, cols), BF16)] * count
    return specs, shapes


def grad_out_part(mx, grad_own, grad_pair, act, split):
    toks = grad_own.shape[0]
    cols = act.shape[1]
    specs, shapes = block_outs(split, cols)

    def body(mx_ref, go, gp, a, *rest):
        outs, (gt, scratch) = rest[:-2], rest[-2:]

        @pl.when(pl.program_id(0) == 0)
        def _():
            gt[:, :toks] = go[...].T
            gt[:, toks:] = gp[...].T

        acc = jnp.dot(gt[...], a[...], preferred_element_type=F32)
        store_blocks(mx_ref[0], acc, scratch, outs)

    return pl.pallas_call(
        body,
        grid=(cols // FC,),
        in_specs=[
            pl.BlockSpec(memory_space=pltpu.SMEM),
            whole((toks, DS)),
            whole((toks, DS)),
            pl.BlockSpec((2 * toks, FC), lambda j: (0, j)),
        ],
        out_specs=specs,
        out_shape=shapes,
        scratch_shapes=[pltpu.VMEM((DS, 2 * toks), BF16), pltpu.VMEM((DS, FC), BF16)],
        compiler_params=LIGHT,
        cost_estimate=TINY,
        name="grad_out",
    )(mx, grad_own, grad_pair, act)


def grad_in_part(mx, grad_own, grad_pair, w_out, slope, normed_t, split):
    toks = grad_own.shape[0]
    cols = w_out.shape[-1]
    specs, shapes = block_outs(split, cols)

    def body(mx_ref, go, gp, w, sl, nrm, *rest):
        outs, (pre, scratch) = rest[:-2], rest[-2:]
        for part, off in ((go, 0), (gp, toks)):
            act_grad = jnp.dot(part[...], flat(w), preferred_element_type=F32)
            pre[off : off + toks, :] = (act_grad * sl[off : off + toks, :]).astype(BF16)
        acc = jnp.dot(nrm[...], pre[...], preferred_element_type=F32)
        store_blocks(mx_ref[0], acc, scratch, outs)

    return pl.pallas_call(
        body,
        grid=(cols // FC,),
        in_specs=[
            pl.BlockSpec(memory_space=pltpu.SMEM),
            whole((toks, DS)),
            whole((toks, DS)),
            weight_spec(w_out, 1, FC),
            pl.BlockSpec((2 * toks, FC), lambda j: (0, j)),
            whole((DS, 2 * toks)),
        ],
        out_specs=specs,
        out_shape=shapes,
        scratch_shapes=[pltpu.VMEM((2 * toks, FC), BF16), pltpu.VMEM((DS, FC), BF16)],
        compiler_params=LIGHT,
        cost_estimate=TINY,
        name="grad_in",
    )(mx, grad_own, grad_pair, w_out, slope, normed_t)


def after(value, *deps):
    return lax.optimization_barrier((value,) + deps)[0]


def together(*values):
    return lax.optimization_barrier(values)


def nt(left, right):
    return lax.dot_general(left, right, (((1,), (1,)), ((), ())), preferred_element_type=F32)


def tn(left, right):
    return lax.dot_general(
        left, right, (((0,), (0,)), ((), ())), preferred_element_type=F32
    ).astype(BF16)


def pair_shards(teacher_feats, t_gain, t_bias, projection, student_in, s_gain, w_in, w_out):
    mx = lax.axis_index("mx")
    g = lax.axis_index("group")
    patch_all, image_loc, feat_loc = teacher_feats.shape
    patch_loc = patch_all // 4
    toks = patch_loc * image_loc
    tokens = PATCHES * image_loc * 4
    w_out = w_out.T
    rows, cols = w_in.shape
    half = rows // 2
    mine, other = g * half, (1 - g) * half

    mx1 = mx.reshape(1).astype(jnp.int32)

    def my_half(w):
        return lax.dynamic_slice(w, (mine, 0), (half, cols))

    z_send = jnp.concatenate([my_half(w_in), my_half(w_out)], axis=0)
    z_g = swap(z_send, "my", 2)
    near = lax.all_gather(jnp.concatenate([w_in, w_out], axis=0), "mx", axis=0, tiled=True)
    near = near.reshape(4, 2, rows, cols)

    feats = teacher_feats.reshape(4 * toks, feat_loc)
    student = student_in.reshape(toks, DS)
    normed_own = student_norm(after(student, z_send), s_gain.reshape(1, DS))
    normed_pair = swap(normed_own, "my", 1)
    sums = teacher_sums(after(feats, normed_own))
    sums = lax.psum(sums[:2], "mx")
    gain = t_gain.astype(F32).reshape(1, feat_loc)
    bias = t_bias.astype(F32).reshape(1, feat_loc)
    parts = target_parts(mx1, (3, 2, 1, 0), feats, sums, gain, bias, projection)
    q3, q2, q1, q0, z_g, normed_pair = together(*parts, z_g, normed_pair)

    d_g = swap(z_g, "mx", 2)
    z_o = swap(z_g, "group", 1)
    zgc = swap(z_g, "mx", 1)
    q3c = swap(q3, "mx", 1)
    pre_near, act_near = forward_part(normed_own, normed_pair, near)
    near_share = branch_near_part(act_near, near)
    pre_near, act_near, near_share, d_g, z_o, zgc, q3c = together(
        pre_near, act_near, near_share, d_g, z_o, zgc, q3c
    )
    in_do = swap(d_g[:half], "group", 1)
    out_do = swap(z_o[half:], "mx", 2)
    zoc, dgc = swap(z_o, "mx", 1), swap(d_g, "mx", 1)
    t2 = (q2.astype(F32) + q3c.astype(F32)).astype(BF16)
    in_do, out_do, zoc, dgc, t2 = together(in_do, out_do, zoc, dgc, t2)
    in_doc, out_doc = swap(in_do, "mx", 1), swap(out_do, "mx", 1)
    in_doc, out_doc = together(in_doc, out_doc)

    def far_rows(first, d_o, d_oc):
        out = []
        for part, part_c, block, off, at in (
            (z_g, zgc, 0, mine, first),
            (z_o, zoc, 0, other, first),
            (d_g, dgc, 2, mine, first),
            (d_o, d_oc, 2, other, 0),
        ):
            out.append((part, at, half, (mx ^ block) * rows + off))
            out.append((part_c, at, half, (mx ^ block ^ 1) * rows + off))
        return out

    target_x = swap(after(t2, in_doc), "mx", 2)
    q1c = swap(after(q1, in_doc), "mx", 1)
    pre_far, act_far = forward_pieces(normed_own, normed_pair, far_rows(0, in_do, in_doc))
    pre_far, act_far, q1c = together(pre_far, act_far, q1c)
    out_rows = far_rows(half, out_do, out_doc)
    t0 = q0.astype(F32) + q1c.astype(F32)

    branch_pair = branch_pieces(near_share, act_far, out_rows, 1, BF16)
    branch_recv = swap(branch_pair, "my", 1)
    out_far = assemble([(p, at, n, after(o, branch_pair)) for p, at, n, o in out_rows], DS)
    branch_own = branch_part(near_share, act_far, out_far, 0, F32)
    branch_own, target_x = together(branch_own, target_x)
    slope_far = gelu_slope(after(pre_far, branch_own))
    branch_recv = after(branch_recv, slope_far)

    target = t0 + target_x.astype(F32)
    residue = student.astype(F32) + (branch_own + branch_recv.astype(F32)) - target
    grad_own = (residue / jnp.sqrt(jnp.float32(tokens))).astype(BF16)
    loss = jnp.broadcast_to(jnp.sum(residue * residue), (8, 128))
    grad_own, loss = lax.optimization_barrier((grad_own, loss))
    grad_pair = swap(grad_own, "my", 1)
    for bit in (1, 2):
        loss = loss + swap(loss, "mx", bit)
    slope_near = gelu_slope(after(pre_near, grad_own))
    normed_t = jnp.concatenate([after(normed_own, slope_near).T, normed_pair.T], axis=1)
    grad_pair, loss, slope_near, normed_t = together(grad_pair, loss, slope_near, normed_t)

    o0, o1, o2, o3 = grad_out_part(mx1, grad_own, grad_pair, act_far, True)
    got2, got0 = swap(o3, "mx", 1), swap(o1, "mx", 1)
    early = rows // 48 * 16
    h0, h1 = slice(0, early), slice(early, rows)
    s2_out = [(o2[c].astype(F32) + got2[c].astype(F32)).astype(BF16) for c in (h0, h1)]
    x_out = [swap(v, "mx", 2) for v in s2_out]
    n0, n1, n2, n3 = grad_out_part(mx1, after(grad_own, *s2_out), grad_pair, act_near, True)
    n0, n1, n2, n3, x_out0, got0 = together(n0, n1, n2, n3, x_out[0], got0)

    def last(keep, got, x):
        return (keep.astype(F32) + got.astype(F32) + x.astype(F32)).astype(BF16)

    f0 = last(o0[h0], got0[h0], x_out0)
    f_out0 = swap(f0, "my", 2)
    gn2, gn0 = swap(after(n3, f0), "mx", 1), swap(after(n1, f0), "mx", 1)
    i0, i1, i2, i3 = grad_in_part(
        mx1, after(grad_own, f0), grad_pair, out_far, slope_far, normed_t, True
    )
    i0, i1, i2, i3, x_out1, gn2, gn0, f_out0 = together(
        i0, i1, i2, i3, x_out[1], gn2, gn0, f_out0
    )
    f1 = last(o0[h1], got0[h1], x_out1)
    f_out1, f_out2 = (swap(f1[c], "my", 2) for c in (slice(0, 64), slice(64, None)))
    gin2, gin0 = swap(i3, "mx", 1), swap(i1, "mx", 1)
    loss_z = swap(after(loss, f1), "my", 1)
    s2_on = (n2.astype(F32) + gn2.astype(F32)).astype(BF16)
    gin2, gin0, s2_on, loss_z, f_out1 = together(gin2, gin0, s2_on, loss_z, f_out1)
    loss = loss + loss_z
    s2_in = (i2.astype(F32) + gin2.astype(F32)).astype(BF16)
    x_in = swap(s2_in, "mx", 2)
    x_on = swap(after(s2_on, s2_in), "mx", 2)
    m0, m1, m2, m3 = grad_in_part(
        mx1, after(grad_own, s2_on, s2_in), grad_pair, near, slope_near, normed_t, True
    )
    m0, m1, m2, m3, x_in, f_out2 = together(m0, m1, m2, m3, x_in, f_out2)
    f2 = [last(i0[c], gin0[c], x_in[c]) for c in (h0, h1)]
    f_in = [swap(v, "my", 2) for v in f2]
    gm2, gm0 = swap(after(m3, *f2), "mx", 1), swap(after(m1, *f2), "mx", 1)
    loss_z = swap(after(loss, *f2), "my", 2)
    gm2, gm0, x_on, f_in0, loss_z = together(gm2, gm0, x_on, f_in[0], loss_z)
    mse_loss = (loss + loss_z)[0, :1] / (tokens * DS)
    s2_mn = (m2.astype(F32) + gm2.astype(F32)).astype(BF16)
    x_mn = swap(s2_mn, "mx", 2)
    grad_out_near = n0.astype(F32) + gn0.astype(F32) + x_on.astype(F32)
    grad_in_near = m0.astype(F32) + gm0.astype(F32) + x_mn.astype(F32)
    f_out = jnp.concatenate([f_out0, f_out1, f_out2], axis=0)
    f_in = jnp.concatenate([f_in0, f_in[1]], axis=0)
    grad_out = (grad_out_near + f_out.astype(F32)).T
    grad_in = grad_in_near + f_in.astype(F32)
    return (mse_loss, grad_in, grad_out)


def shards(teacher_feats, t_gain, t_bias, projection, student_in, s_gain, w_in, w_out):
    patch_all, image_loc, feat_loc = teacher_feats.shape
    mx_count = lax.axis_size("mx")
    my_count = lax.axis_size("my")
    patch_loc = patch_all // mx_count
    features = teacher_feats.astype(jnp.float32)
    feature_sum, squares = lax.psum(
        (jnp.sum(features, axis=2), jnp.sum(features * features, axis=2)), "mx"
    )
    row_mean = feature_sum / DT
    variance = squares / DT - row_mean * row_mean
    normed_teacher = (
        (features - row_mean[..., None])
        * lax.rsqrt(variance + epsilon)[..., None]
        * t_gain.astype(jnp.float32)
        + t_bias.astype(jnp.float32)
    ).astype(jnp.bfloat16)
    flattened = normed_teacher.reshape(patch_loc * lax.axis_size("mx") * image_loc, feat_loc)
    target = lax.psum_scatter(
        jnp.dot(flattened, projection, preferred_element_type=jnp.float32)
        .reshape(patch_loc * lax.axis_size("mx"), image_loc, DS)
        .astype(jnp.bfloat16),
        "mx",
        scatter_dimension=0,
        tiled=True,
    ).astype(jnp.float32)
    student_f32 = student_in.astype(jnp.float32)
    student_mean = jnp.sum(student_f32, axis=2, keepdims=True) / DS
    student_square = jnp.sum(student_f32 * student_f32, axis=2, keepdims=True) / DS
    normed = (
        (student_f32 - student_mean)
        * lax.rsqrt(student_square - student_mean * student_mean + epsilon)
        * s_gain
    ).astype(jnp.bfloat16)
    gathered = lax.all_gather(normed, "my", axis=1, tiled=True)
    rows_all = patch_loc * image_loc * my_count
    normed_flat = gathered.reshape(rows_all, DS)
    preact = jnp.dot(
        normed_flat,
        lax.all_gather(w_in, "mx", axis=0, tiled=True),
        preferred_element_type=jnp.float32,
    )
    activation = gelu_value(preact).astype(jnp.bfloat16)
    w_out_full = lax.all_gather(w_out, "mx", axis=1, tiled=True)
    branch_part = jnp.dot(activation, w_out_full, preferred_element_type=jnp.float32).reshape(
        patch_loc, image_loc * my_count, DS
    )
    branch = lax.psum_scatter(
        branch_part.astype(jnp.bfloat16), "my", scatter_dimension=1, tiled=True
    ).astype(jnp.float32)
    residue = student_f32 + branch - target
    tokens = PATCHES * image_loc * my_count
    squared_sum = lax.psum(jnp.sum(residue * residue), ("mx", "my"))
    mse_loss = jnp.reshape(squared_sum / (tokens * DS), (1,))
    grad_output = (residue / jnp.sqrt(jnp.float32(tokens))).astype(jnp.bfloat16)
    grad_rows = lax.all_gather(grad_output, "my", axis=1, tiled=True).reshape(rows_all, DS)
    grad_act = lax.dot_general(
        grad_rows, w_out_full, (((1,), (1,)), ((), ())), preferred_element_type=jnp.float32
    )
    grad_pre = (grad_act * gelu_slope(preact)).astype(jnp.bfloat16)
    part_in = lax.dot_general(
        normed_flat, grad_pre, (((0,), (0,)), ((), ())), preferred_element_type=jnp.float32
    )
    part_out = lax.dot_general(
        activation, grad_rows, (((0,), (0,)), ((), ())), preferred_element_type=jnp.float32
    )
    grad_in = lax.psum_scatter(
        part_in.astype(jnp.bfloat16), "mx", scatter_dimension=0, tiled=True
    ).astype(jnp.float32)
    grad_out = lax.psum_scatter(
        part_out.astype(jnp.bfloat16), "mx", scatter_dimension=1, tiled=True
    ).astype(jnp.float32)
    return (mse_loss, grad_in, grad_out)


def solution(mesh):
    in_specs = (
        P(None, ("group", "my"), "mx"),
        P("mx"),
        P("mx"),
        P("mx", None),
        P("mx", ("group", "my"), None),
        P(),
        P("mx", "my"),
        P("my", "mx"),
    )
    out_specs = (P("group"), P(("group", "mx"), "my"), P(("group", "my"), "mx"))
    pairs = mesh.shape["group"] == 2 and mesh.shape["mx"] == 4 and mesh.shape["my"] == 4
    body = pair_shards if pairs else shards
    return jax.shard_map(body, mesh=mesh, in_specs=in_specs, out_specs=out_specs, check_vma=False)
```
